256 devices in a mesh: segment: 2 (over core), dp: 16 (over y_lo, z), tensor: 8 (over x, y_hi).
Axes of the slice: x: 4, y: 4 (y_hi: 2, y_lo: 2; y = y_hi * 2 + y_lo), z: 8, core: 2. Of those that a mesh axis runs over, the one named last changes fastest.
Arguments:
- tokens: bfloat16 [256, 5120], P('dp'), may hold values from -12 to 12
- cotangent: bfloat16 [256, 5120], P('dp'), may hold values from -6 to 6
- gains: float32 [2, 5120], P('segment'), may hold values from 0.1 to 1.9
- w_gate: bfloat16 [2, 5120, 27648], P('segment', 'dp', 'tensor'), may hold values from -0.078125 to 0.078125
- w_up: bfloat16 [2, 5120, 27648], P('segment', 'dp', 'tensor'), may hold values from -0.078125 to 0.078125
- w_down: bfloat16 [2, 5120, 27648], P('segment', 'dp', 'tensor'), may hold values from -0.0390625 to 0.0390625
Outputs:
- acts: bfloat16 [2, 256, 5120], P('segment', 'dp')
- grads: bfloat16 [2, 256, 5120], P('segment', 'dp')
The draws below stay inside these ranges and needn't reach their ends.
All inputs are finite; a program needn't handle non-finite values.
Results may differ from the reference program's by a relative error of at most 0.04.
Values may be sent and summed in bfloat16 or wider, within the bound.
A program may use at most 64 MiB of HBM per device.

```python
import math
import jax
import jax.numpy as jnp
from jax import lax

D = 5120
FF = 27648
TOKENS = 256
N_DP = 16


def draw_tokens(key, part):
    noise_key, row_key = jax.random.split(key, 2)
    row_scale = jnp.exp(jax.random.uniform(row_key, (TOKENS, 1), jnp.float32, math.log(0.3), math.log(3.0)))
    noise_values = jnp.clip(jax.random.normal(noise_key, (TOKENS, D), jnp.float32), -4.0, 4.0)
    return (noise_values * row_scale).astype(jnp.bfloat16)


def level_of(stream_key, dims, cuts, least, top_value):
    def one(dim, shards_of):
        draws = jax.random.uniform(jax.random.fold_in(jax.random.fold_in(stream_key, 6), dim), (shards_of,), jnp.float32, least / len(cuts), top_value / len(cuts))
        return jnp.repeat(jnp.exp(draws), dims[dim] // shards_of).reshape((-1,) + (1,) * (len(dims) - dim - 1))

    gain = one(*cuts[0])
    for cut in cuts[1:]:
        gain = gain * one(*cut)
    return gain


def scatter_about(stream_key, shape, scale, most, pieces=(), held_as=jnp.bfloat16):
    values = scale * jax.random.normal(stream_key, shape, jnp.float32)
    if pieces:
        values = values * level_of(stream_key, shape, pieces, -0.22, 0.18)
    return jnp.clip(values, -most, most).astype(held_as)


def setup_inputs(seed: int = 0) -> dict:
    seeds = jax.random.split(jax.random.key(seed), 7)
    tokens = draw_tokens(jax.random.fold_in(seeds[6], 71), 0)
    cotangent = scatter_about(seeds[1], (TOKENS, D), 1.0, 6.0, ((0, 16),))
    gains = jnp.clip(1.0 + 0.18 * jax.random.normal(seeds[2], (2, D), jnp.float32), 0.1, 1.9)
    w_gate = scatter_about(seeds[3], (2, D, FF), D ** -0.5, 0.078125, ((0, 2), (1, 16), (2, 8)))
    w_up = scatter_about(seeds[4], (2, D, FF), D ** -0.5, 0.078125, ((0, 2), (1, 16), (2, 8)))
    w_down = scatter_about(seeds[5], (2, D, FF), FF ** -0.5, 0.0390625, ((0, 2), (1, 16), (2, 8)))
    return dict(tokens=tokens, cotangent=cotangent, gains=gains, w_gate=w_gate, w_up=w_up, w_down=w_down)


EPSILON = 1e-06

def normalize(values):
    wide = values.astype(jnp.float32)
    inverse = lax.rsqrt(lax.optimization_barrier(jnp.mean(wide * wide, axis=1, keepdims=True)) + EPSILON)
    return (wide, wide * inverse, inverse)

def contract_last(left, right):
    return lax.dot_general(left, right, (((1,), (1,)), ((), ())), preferred_element_type=jnp.float32)

def blocked_product(left, right):
    width = left.shape[1] // N_DP
    total = jnp.zeros((left.shape[0], right.shape[1]), jnp.float32)
    for block in range(N_DP):
        piece = jnp.dot(left[:, block * width:(block + 1) * width], right[block * width:(block + 1) * width, :], preferred_element_type=jnp.float32)
        rounded = lax.optimization_barrier(piece.astype(jnp.bfloat16))
        total = total + rounded.astype(jnp.float32)
    return total

def sublayer_forward(values, gain_row, gate_weight, up_weight, down_weight):
    wide, unit, inverse = normalize(values)
    normed = (unit * gain_row[None, :]).astype(jnp.bfloat16)
    gate_pre = blocked_product(normed, gate_weight)
    up_pre = blocked_product(normed, up_weight)
    hidden = (jax.nn.silu(gate_pre) * up_pre).astype(jnp.bfloat16)
    branch_out = contract_last(hidden, down_weight)
    return ((wide + branch_out).astype(jnp.bfloat16), gate_pre.astype(jnp.bfloat16), up_pre.astype(jnp.bfloat16))

def sublayer_backward(values, gain_row, gate_weight, up_weight, down_weight, stash_gate, stash_up, incoming):
    wide, unit, inverse = normalize(values)
    d_hidden = blocked_product(incoming, down_weight)
    gate_pre = stash_gate.astype(jnp.float32)
    up_pre = stash_up.astype(jnp.float32)
    sigmoid_gate = jax.nn.sigmoid(gate_pre)
    d_gate = (d_hidden * up_pre * sigmoid_gate * (1.0 + gate_pre * (1.0 - sigmoid_gate))).astype(jnp.bfloat16)
    d_up = (d_hidden * gate_pre * sigmoid_gate).astype(jnp.bfloat16)
    d_normed = contract_last(d_gate, gate_weight) + contract_last(d_up, up_weight)
    weighted = d_normed * gain_row[None, :]
    projection = lax.optimization_barrier(jnp.mean(weighted * unit, axis=1, keepdims=True))
    return (incoming.astype(jnp.float32) + inverse * (weighted - unit * projection)).astype(jnp.bfloat16)

def reference(tokens, cotangent, gains, w_gate, w_up, w_down):
    early_out, early_gate, early_up = sublayer_forward(tokens, gains[0], w_gate[0], w_up[0], w_down[0])
    late_out, late_gate, late_up = sublayer_forward(early_out, gains[1], w_gate[1], w_up[1], w_down[1])
    d_early = sublayer_backward(early_out, gains[1], w_gate[1], w_up[1], w_down[1], late_gate, late_up, cotangent)
    d_tokens = sublayer_backward(tokens, gains[0], w_gate[0], w_up[0], w_down[0], early_gate, early_up, d_early)
    return (jnp.stack([early_out, late_out]), jnp.stack([d_tokens, d_early]))
```

```python
import functools

import jax
import jax.numpy as jnp
from jax import lax
from jax.experimental import pallas as pl
from jax.experimental.pallas import tpu as pltpu
from jax.sharding import PartitionSpec as P

EPSILON = 1e-06
MESH = pl.DeviceIdType.MESH
F32 = jnp.float32
BF16 = jnp.bfloat16
Z = 8
ORDER = (4, 3, -3, 2, -2, 1, -1, 0)


def halves(tiles):
    first = (tiles + 1) // 2
    return ((0, first * 128, 0), (first * 128, (tiles - first) * 128, 1))


def rows_of(block):
    return block.reshape(-1, block.shape[-1])


def kernel(
    sizes,
    blocks,
    gain_here,
    gain_all,
    wg_hbm,
    wu_hbm,
    wd_hbm,
    acts,
    grads,
    wg,
    wu,
    wd,
    tin,
    pin,
    xg,
    pg,
    pu,
    pd,
    gu_y,
    gu_ring_y,
    gu_ring_z,
    gu_out,
    gu_fin,
    dh_y,
    dh_ring_y,
    dh_ring_z,
    dh_out,
    dh_fin,
    stash_g,
    stash_u,
    dh_sum,
    hid,
    dg,
    du,
    acc,
    t_out,
    t_in,
    made,
    st_out,
    st_in,
    rows_early,
    rows_back,
    rows_last,
    inv,
    w_sem,
    in_sem,
    gu_sem,
    gu_ysem,
    dh_sem,
    dh_ysem,
    ag_sem,
    ag_ysem,
    t_sem,
    p_sem,
    st_sem,
    row_send,
    row_recv,
    fwd_sem,
    go_sem,
):
    dp_count, tensor_count, rows, width, hidden = sizes
    per = dp_count // tensor_count
    tiles = hidden // 128
    cut = ((tiles * 5 + 8) // 9) * 128
    step_cols = 384
    seg = lax.axis_index("segment")
    i = lax.axis_index("dp")
    j = lax.axis_index("tensor")
    y = i // Z
    m = lax.rem(i, Z)
    across = (seg, (1 - y) * Z + m, j)
    side = (
        (seg, y * Z + lax.rem(m + Z - 1, Z), j),
        (seg, y * Z + lax.rem(m + 1, Z), j),
    )
    partner = (1 - seg, i, j)

    def at(offset):
        return lax.rem(m + offset + Z, Z)

    def dp_peer(r):
        return (seg, lax.rem(i + r, dp_count), j)

    def tensor_at(r):
        return lax.rem(j + r, tensor_count)

    def send(src, dst, send_sem, recv_sem, to):
        copy = pltpu.make_async_remote_copy(
            src_ref=src,
            dst_ref=dst,
            send_sem=send_sem,
            recv_sem=recv_sem,
            device_id=to,
            device_id_type=MESH,
        )
        copy.start()
        return copy

    def arrived(ref, sem):
        pltpu.make_async_copy(ref, ref, sem).wait()

    barrier = pltpu.get_barrier_semaphore()
    for r in range(1, dp_count):
        pl.semaphore_signal(barrier, inc=1, device_id=dp_peer(r), device_id_type=MESH)
    for r in range(1, tensor_count):
        pl.semaphore_signal(barrier, inc=1, device_id=(seg, i, tensor_at(r)), device_id_type=MESH)
    pl.semaphore_signal(barrier, inc=1, device_id=partner, device_id_type=MESH)
    loads = [
        pltpu.make_async_copy(src.at[0], dst, w_sem.at[n])
        for n, (src, dst) in enumerate(((wg_hbm, wg), (wu_hbm, wu), (wd_hbm, wd)))
    ]
    for load in loads:
        load.start()
    tin[i] = blocks[i]
    pl.semaphore_wait(barrier, dp_count - 1 + tensor_count - 1 + 1)

    entry = []
    for r in range(1, dp_count):
        to = lax.rem(i + r, dp_count)
        entry.append(
            send(blocks.at[to], tin.at[i], in_sem.at[0, r], in_sem.at[1, r], (seg, to, j))
        )

    def write_inverse(source):
        def add(b, total):
            v = source[b].astype(F32)
            return total + v * v

        squares = lax.fori_loop(0, dp_count, add, jnp.zeros((rows, width), F32))
        mean = jnp.sum(squares, axis=1, keepdims=True) / (dp_count * width)
        inv[...] = jnp.broadcast_to(lax.rsqrt(mean + EPSILON), (rows, 128))

    def spread(x, weight, out, c0, count):
        span = step_cols if count % step_cols == 0 else 128

        def one(n, carry):
            c = pl.multiple_of(c0 + n * span, 128)
            v = jnp.dot(x, weight[:, pl.ds(c, span)], preferred_element_type=F32)
            out[:, :, :, pl.ds(c, span)] = v.astype(BF16).reshape(2, Z, rows, span)
            return carry

        lax.fori_loop(0, count // span, one, 0)

    def fold(left, weight, first):
        span = step_cols

        def one(n, carry):
            c = pl.multiple_of(n * span, 128)
            v = lax.dot_general(
                rows_of(left[:, :, :, pl.ds(c, span)]),
                weight[:, pl.ds(c, span)],
                (((1,), (1,)), ((), ())),
                preferred_element_type=F32,
            )
            acc[...] += v
            return carry

        if first:
            acc[...] = jnp.zeros_like(acc)
        lax.fori_loop(0, hidden // span, one, 0)

    class Ring:
        def __init__(self, own, land, pieces, sem):
            self.own, self.land, self.pieces, self.sem = own, land, pieces, sem
            self.last, self.sent = {}, []

        def cols(self, t, d, k):
            c0, w, _ = self.pieces[k]
            lead = (slice(None),) * (len(self.land.shape) - 3)
            return (t, d, *lead, pl.ds(c0, w))

        def push(self, t, d, k, src):
            copy = send(
                src,
                self.land.at[self.cols(t, d, k)],
                self.sem.at[0, t, d, k],
                self.sem.at[1, t, d, k],
                side[d],
            )
            self.last[t, d, k] = copy
            self.sent.append(copy)

        def step(self, t):
            for k, (c0, w, anti) in enumerate(self.pieces):
                for d in (0, 1):
                    dest = at(t - 4 if d == 0 else 4 - t)
                    if t == 0 and d != anti:
                        continue
                    if t == 0 or (t == 1 and d != anti):
                        self.push(t, d, k, self.own(dest, c0, w))
                        continue
                    self.last[t - 1, d, k].wait_recv()
                    here = self.land.at[self.cols(t - 1, d, k)]
                    here[...] = here[...] + self.own(dest, c0, w)[...]
                    self.push(t, d, k, here)

        def finish(self):
            for k in range(len(self.pieces)):
                for d in (0, 1):
                    self.last[3, d, k].wait_recv()

    def reduce_scatter(py, y0, wy, pz, z0, wz, by, ring_y, ring_z, z_out, z_fin, sem, ysem, fill_y, fill_z):
        fill_y()
        swaps = [
            send(
                py.at[1 - y, at(off), :, pl.ds(y0, wy)],
                by.at[at(off)],
                ysem.at[0, n],
                ysem.at[1, n],
                across,
            )
            for n, off in enumerate(ORDER)
        ]
        fill_z()
        over_z = Ring(
            lambda dest, c0, w: pz.at[:, dest, :, pl.ds(z0 + c0, w)], ring_z, halves(wz // 128), sem.at[0]
        )
        over_y = Ring(lambda dest, c0, w: by.at[dest, :, pl.ds(c0, w)], ring_y, halves(wy // 128), sem.at[1])

        def pair(n):
            swaps[n].wait_recv()
            zd = at(ORDER[n])
            by[zd] = by[zd] + py[y, zd, :, pl.ds(y0, wy)]

        over_z.step(0)
        pair(0)
        over_y.step(0)
        for t in (1, 2, 3):
            over_z.step(t)
            pair(2 * t - 1)
            pair(2 * t)
            over_y.step(t)
        over_z.finish()
        z_out[...] = (
            pz[1 - y, m, :, pl.ds(z0, wz)].astype(F32)
            + ring_z[3, 0, 1 - y].astype(F32)
            + ring_z[3, 1, 1 - y].astype(F32)
        ).astype(BF16)
        last = send(z_out, z_fin, ysem.at[0, Z], ysem.at[1, Z], across)
        pair(7)
        over_y.finish()
        last.wait_recv()
        for copy in (*swaps, *over_z.sent, *over_y.sent, last):
            copy.wait_send()

    def y_total(by, ring_y, c, span):
        cols = pl.ds(c, span)
        return (
            by[m, :, cols].astype(F32) + ring_y[3, 0, :, cols].astype(F32) + ring_y[3, 1, :, cols].astype(F32)
        )

    def z_total(pz, z0, ring_z, z_fin, c, span):
        cols = pl.ds(c, span)
        return (
            pz[y, m, :, pl.ds(z0 + c, span)].astype(F32)
            + ring_z[3, 0, y, :, cols].astype(F32)
            + ring_z[3, 1, y, :, cols].astype(F32)
            + z_fin[:, cols].astype(F32)
        )

    def scatter_hidden_grads(source):
        x = rows_of(source[...])
        reduce_scatter(
            pd, 0, cut, pd, cut, hidden - cut, dh_y, dh_ring_y, dh_ring_z, dh_out, dh_fin, dh_sem, dh_ysem,
            lambda: spread(x, wd, pd, 0, cut),
            lambda: spread(x, wd, pd, cut, hidden - cut),
        )
        dh_sum[:, pl.ds(0, cut)] = y_total(dh_y, dh_ring_y, 0, cut)
        dh_sum[:, pl.ds(cut, hidden - cut)] = z_total(pd, cut, dh_ring_z, dh_fin, 0, hidden - cut)

    def all_gather(a, a0, wa, b, b0, wb, sem, ysem):
        ca, cb = pl.ds(a0, wa), pl.ds(b0, wb)
        sent, over_a, over_b, cross = [], {}, {}, []

        def push_a(t, d, origin):
            part = a.at[y, origin, :, ca]
            over_a[t, d] = send(part, part, sem.at[0, 0, t, d], sem.at[0, 1, t, d], side[d])
            sent.append(over_a[t, d])

        def push_b(t, d, origin):
            part = b.at[:, origin, :, cb]
            over_b[t, d] = send(part, part, sem.at[1, 0, t, d], sem.at[1, 1, t, d], side[d])
            sent.append(over_b[t, d])

        def cross_a(origin):
            part = a.at[y, origin, :, ca]
            n = len(cross)
            cross.append(send(part, part, ysem.at[0, n], ysem.at[1, n], across))

        mine = b.at[y, m, :, cb]
        first = send(mine, mine, ysem.at[0, Z], ysem.at[1, Z], across)
        push_a(0, 0, m)
        push_a(0, 1, m)
        cross_a(m)
        first.wait_recv()
        push_b(0, 0, m)
        push_b(0, 1, m)
        for t in (1, 2, 3, 4):
            for over, push, anti in ((over_a, push_a, 0), (over_b, push_b, 1)):
                for d in (0, 1):
                    if t == 4 and d != anti:
                        continue
                    over[t - 1, d].wait_recv()
                    origin = at(t if d == 0 else -t)
                    if t < 3 or (t == 3 and d == anti):
                        push(t, d, origin)
                    if over is over_a:
                        cross_a(origin)
        for copy in cross:
            copy.wait_recv()
        return [first, *sent, *cross]

    def drain(copies):
        for copy in copies:
            copy.wait_send()

    def tensor_sum(turn):
        t_out[turn] = acc[...].reshape(tensor_count, per, rows, width).astype(BF16)
        copies = []
        for r in range(1, tensor_count):
            jd = tensor_at(r)
            copies.append(
                send(
                    t_out.at[turn, jd],
                    t_in.at[turn, r - 1],
                    t_sem.at[turn, 0, r],
                    t_sem.at[turn, 1, r],
                    (seg, i, jd),
                )
            )
        total = t_out[turn, j].astype(F32)
        for r in range(1, tensor_count):
            copies[r - 1].wait_recv()
            total = total + t_in[turn, r - 1].astype(F32)
        return total, copies

    def to_partner_segment(src):
        copies = []
        for r in range(tensor_count):
            copies.append(
                send(
                    src,
                    pin.at[pl.ds(per * j, per)],
                    p_sem.at[0, r],
                    p_sem.at[1, r],
                    (1 - seg, i, tensor_at(r)),
                )
            )
        return copies

    def from_partner_segment():
        for r in range(tensor_count):
            arrived(pin.at[pl.ds(0, per)], p_sem.at[1, r])

    def to_rows(src, land, kind, to_seg, crosses):
        for r in range(tensor_count):
            for q in range(per):
                to = (to_seg, per * j + q, tensor_at(r))
                s = row_send.at[kind, r, q]
                if crosses or r > 0:
                    send(src.at[q], land.at[i], s, row_recv.at[kind, i], to)
                    continue
                own = i == per * j + q

                @pl.when(own)
                def _():
                    land[i] = src[q]

                @pl.when(jnp.logical_not(own))
                def _():
                    send(src.at[q], land.at[i], s, row_recv.at[kind, i], to)

    def drain_rows(src, kind, crosses):
        for r in range(tensor_count):
            for q in range(per):
                if crosses or r > 0:
                    arrived(src.at[q], row_send.at[kind, r, q])
                    continue

                @pl.when(i != per * j + q)
                def _():
                    arrived(src.at[q], row_send.at[kind, r, q])

    def rows_arrived(land, kind, crosses):
        def one(s, carry):
            if crosses:
                arrived(land.at[s], row_recv.at[kind, s])
            else:

                @pl.when(jnp.logical_or(s != i, i // per != j))
                def _():
                    arrived(land.at[s], row_recv.at[kind, s])

            return carry

        lax.fori_loop(0, dp_count, one, 0)

    early = seg == 0
    late = seg == 1
    here = pl.ds(per * j, per)
    gain_row = gain_here[...]

    for copy in entry:
        copy.wait_recv()

    def scale(source):
        xg[...] = (rows_of(source[...]).astype(F32) * gain_row).astype(BF16)

    @pl.when(early)
    def _():
        scale(tin)

    @pl.when(late)
    def _():
        loads[2].wait()
        pl.semaphore_wait(go_sem, 1)
        scatter_hidden_grads(tin)
        from_partner_segment()
        scale(pin)

    def fill_gate():
        loads[0].wait()
        spread(xg[...], wg, pg, 0, hidden)

    def fill_up():
        loads[1].wait()
        spread(xg[...], wu, pu, 0, hidden)

    reduce_scatter(
        pg, 0, hidden, pu, 0, hidden, gu_y, gu_ring_y, gu_ring_z, gu_out, gu_fin, gu_sem, gu_ysem, fill_gate, fill_up
    )

    @pl.when(early)
    def _():
        write_inverse(blocks)

    @pl.when(late)
    def _():
        rows_arrived(rows_early, 0, True)
        write_inverse(rows_early)

    def activate(n, carry):
        c = pl.multiple_of(n * step_cols, 128)
        cols = pl.ds(c, step_cols)
        factor = inv[:, 0:1]
        gate = factor * y_total(gu_y, gu_ring_y, c, step_cols)
        up = factor * z_total(pu, 0, gu_ring_z, gu_fin, c, step_cols)
        stash_g[:, cols] = gate.astype(BF16)
        stash_u[:, cols] = up.astype(BF16)
        hid[y, m, :, cols] = (gate * jax.nn.sigmoid(gate) * up).astype(BF16)
        return carry

    lax.fori_loop(0, hidden // step_cols, activate, 0)

    def write_hidden_grads():
        def one(n, carry):
            c = pl.multiple_of(n * step_cols, 128)
            cols = pl.ds(c, step_cols)
            g = stash_g[:, cols].astype(F32)
            u = stash_u[:, cols].astype(F32)
            d = dh_sum[:, cols]
            s = jax.nn.sigmoid(g)
            dg[y, m, :, cols] = (d * u * s * (1.0 + g * (1.0 - s))).astype(BF16)
            du[y, m, :, cols] = (d * g * s).astype(BF16)
            return carry

        lax.fori_loop(0, hidden // step_cols, one, 0)

    a_cols = cut
    b_cols = hidden - cut

    def gather_hidden():
        return all_gather(hid, 0, a_cols, hid, a_cols, b_cols, ag_sem.at[0], ag_ysem.at[0])

    def gather_hidden_grads():
        return all_gather(dg, 0, hidden, du, 0, hidden, ag_sem.at[1], ag_ysem.at[1])

    @pl.when(early)
    def _():
        loads[2].wait()
        gathers = gather_hidden()
        pl.semaphore_signal(go_sem, inc=1, device_id=partner, device_id_type=MESH)
        fold(hid, wd, True)
        total, sums = tensor_sum(0)
        made[0] = (tin[here].astype(F32) + total).astype(BF16)
        handed = to_partner_segment(made.at[0])
        to_rows(made.at[0], rows_early, 0, 1 - seg, True)
        drain(gathers)
        drain(sums)
        drain(handed)
        drain_rows(made.at[0], 0, True)
        from_partner_segment()
        scatter_hidden_grads(pin)
        write_hidden_grads()
        gathers = gather_hidden_grads()
        fold(dg, wg, True)
        fold(du, wu, False)
        total, sums = tensor_sum(1)
        made[1] = total.astype(BF16)
        to_rows(made.at[1], rows_last, 2, seg, False)
        arrived(rows_early, fwd_sem.at[1, 0])
        acts[...] = rows_early[...]
        rows_arrived(rows_back, 1, True)
        back = send(rows_back, rows_back, fwd_sem.at[0, 1], fwd_sem.at[1, 1], partner)
        rows_arrived(rows_last, 2, False)
        factor = inv[:, 0:1]
        project = jnp.zeros((rows, width), F32)
        for b in range(dp_count):
            weighted = rows_last[b].astype(F32) * gain_all[b : b + 1, :]
            project = project + weighted * (blocks[b].astype(F32) * factor)
        mean = jnp.sum(project, axis=1, keepdims=True) / (dp_count * width)
        for b in range(dp_count):
            weighted = rows_last[b].astype(F32) * gain_all[b : b + 1, :]
            unit = blocks[b].astype(F32) * factor
            grads[b] = (rows_back[b].astype(F32) + factor * (weighted - unit * mean)).astype(BF16)
        back.wait_send()
        drain(gathers)
        drain(sums)
        drain_rows(made.at[1], 2, False)

    @pl.when(late)
    def _():
        write_hidden_grads()
        gathers = gather_hidden_grads()
        fold(dg, wg, True)
        fold(du, wu, False)
        total, sums = tensor_sum(0)
        weighted = rows_of(total) * gain_row
        e = rows_of(pin[here]).astype(F32)
        count = per * rows
        both = jnp.concatenate([weighted * e, e * e], axis=0)
        st_out[...] = jnp.zeros_like(st_out)
        st_out[:, pl.ds(0, 2 * count)] = lax.dot_general(
            jnp.ones((8, width), F32),
            both,
            (((1,), (1,)), ((), ())),
            preferred_element_type=F32,
            precision=lax.Precision.HIGHEST,
        )
        stats = [
            send(st_out, st_in.at[r], st_sem.at[0, r], st_sem.at[1, r], dp_peer(r)) for r in range(1, dp_count)
        ]
        tally = st_out[...]
        for r in range(1, dp_count):
            stats[r - 1].wait_recv()
            tally = tally + st_in[r]
        turned = tally.T
        dot_e = turned[0:count, 0:1] / (dp_count * width)
        squares = turned[count : 2 * count, 0:1] / (dp_count * width)
        factor = lax.rsqrt(squares + EPSILON)
        c = rows_of(tin[here]).astype(F32)
        d_in = c + factor * (weighted - e * factor * (factor * dot_e))
        made[0] = d_in.astype(BF16).reshape(per, rows, width)
        handed = to_partner_segment(made.at[0])
        to_rows(made.at[0], rows_back, 1, 1 - seg, True)
        drain(gathers)
        drain(sums)
        drain(stats)
        gathers = gather_hidden()
        fold(hid, wd, True)
        total, sums = tensor_sum(1)
        made[1] = (pin[here].astype(F32) + total).astype(BF16)
        to_rows(made.at[1], rows_last, 2, seg, False)
        ahead = send(rows_early, rows_early, fwd_sem.at[0, 0], fwd_sem.at[1, 0], partner)
        arrived(rows_back, fwd_sem.at[1, 1])
        grads[...] = rows_back[...]
        rows_arrived(rows_last, 2, False)
        acts[...] = rows_last[...]
        ahead.wait_send()
        drain(gathers)
        drain(sums)
        drain(handed)
        drain_rows(made.at[0], 1, True)
        drain_rows(made.at[1], 2, False)

    for copy in entry:
        copy.wait_send()


def solution(mesh):
    dp_count, tensor_count = mesh.shape["dp"], mesh.shape["tensor"]

    def body(tokens, cotangent, gains, w_gate, w_up, w_down):
        rows, model = tokens.shape
        _, width, hidden = w_gate.shape
        per = dp_count // tensor_count
        tiles = hidden // 128
        cut = ((tiles * 5 + 8) // 9) * 128
        rest = hidden - cut
        i = lax.axis_index("dp")
        lead = lax.axis_index("segment") == 0

        def in_blocks(a):
            return a.reshape(rows, dp_count, width).transpose(1, 0, 2)

        blocks = in_blocks(jnp.where(lead, tokens, cotangent))
        gain_all = gains.reshape(dp_count, width)
        gain_here = lax.dynamic_slice(gain_all, (i, 0), (1, width))

        def buf(*shape, dtype=BF16):
            return pltpu.VMEM(shape, dtype)

        block = (dp_count, rows, width)
        wide = (2, Z, rows, hidden)
        dma = pltpu.SemaphoreType.DMA
        scratch = [
            buf(width, hidden),
            buf(width, hidden),
            buf(width, hidden),
            buf(*block),
            buf(*block),
            buf(dp_count * rows, width),
            buf(*wide),
            buf(*wide),
            buf(*wide),
            buf(Z, rows, hidden),
            buf(4, 2, rows, hidden),
            buf(4, 2, 2, rows, hidden),
            buf(rows, hidden),
            buf(rows, hidden),
            buf(Z, rows, cut),
            buf(4, 2, rows, cut),
            buf(4, 2, 2, rows, rest),
            buf(rows, rest),
            buf(rows, rest),
            buf(rows, hidden),
            buf(rows, hidden),
            buf(rows, hidden, dtype=F32),
            buf(*wide),
            buf(*wide),
            buf(*wide),
            buf(dp_count * rows, width, dtype=F32),
            buf(2, tensor_count, per, rows, width),
            buf(2, tensor_count - 1, per, rows, width),
            buf(2, per, rows, width),
            buf(8, 128, dtype=F32),
            buf(dp_count, 8, 128, dtype=F32),
            buf(*block),
            buf(*block),
            buf(*block),
            buf(rows, 128, dtype=F32),
            dma((3,)),
            dma((2, dp_count)),
            dma((2, 2, 4, 2, 2)),
            dma((2, Z + 1)),
            dma((2, 2, 4, 2, 2)),
            dma((2, Z + 1)),
            dma((2, 2, 2, 4, 2)),
            dma((2, 2, Z + 1)),
            dma((2, 2, tensor_count)),
            dma((2, tensor_count)),
            dma((2, dp_count)),
            dma((3, tensor_count, per)),
            dma((3, dp_count)),
            dma((2, 2)),
            pltpu.SemaphoreType.REGULAR,
        ]
        vmem = pl.BlockSpec(memory_space=pltpu.VMEM)
        hbm = pl.BlockSpec(memory_space=pl.ANY)
        acts, grads = pl.pallas_call(
            functools.partial(kernel, (dp_count, tensor_count, rows, width, hidden)),
            out_shape=[jax.ShapeDtypeStruct(block, BF16)] * 2,
            in_specs=[vmem, vmem, vmem, hbm, hbm, hbm],
            out_specs=[vmem, vmem],
            scratch_shapes=scratch,
            compiler_params=pltpu.CompilerParams(collective_id=0, has_side_effects=True),
        )(blocks, gain_here, gain_all, w_gate, w_up, w_down)

        def in_rows(a):
            return a.transpose(1, 0, 2).reshape(1, rows, model)

        return in_rows(acts), in_rows(grads)

    in_specs = (
        P("dp", None),
        P("dp", None),
        P("segment", None),
        P("segment", "dp", "tensor"),
        P("segment", "dp", "tensor"),
        P("segment", "dp", "tensor"),
    )
    out_specs = (P("segment", "dp", None), P("segment", "dp", None))
    return jax.shard_map(body, mesh=mesh, in_specs=in_specs, out_specs=out_specs, check_vma=False)
```

```python
import functools

import jax
import jax.numpy as jnp
from jax import lax
from jax.experimental import pallas as pl
from jax.experimental.pallas import tpu as pltpu
from jax.sharding import PartitionSpec as P

EPSILON = 1e-06
MESH = pl.DeviceIdType.MESH
F32 = jnp.float32
BF16 = jnp.bfloat16
Z = 8
ORDER = (4, 3, -3, 2, -2, 1, -1, 0)


def halves(tiles):
    first = (tiles + 1) // 2
    return ((0, first * 128, 0), (first * 128, (tiles - first) * 128, 1))


def rows_of(block):
    return block.reshape(-1, block.shape[-1])


def kernel(
    sizes,
    tokens_hbm,
    cotangent_hbm,
    gains,
    wg_hbm,
    wu_hbm,
    wd_hbm,
    acts,
    grads,
    given,
    blocks,
    gain_all,
    wg,
    wu,
    wd,
    tin,
    pin,
    xg,
    pg,
    pu,
    pd,
    gu_y,
    gu_ring_y,
    gu_ring_z,
    gu_out,
    gu_fin,
    dh_y,
    dh_ring_y,
    dh_ring_z,
    dh_out,
    dh_fin,
    stash_g,
    stash_u,
    dh_sum,
    hid,
    dg,
    du,
    acc,
    t_out,
    t_in,
    made,
    st_out,
    st_in,
    rows_early,
    rows_back,
    rows_last,
    inv,
    w_sem,
    in_sem,
    gu_sem,
    gu_ysem,
    dh_sem,
    dh_ysem,
    ag_sem,
    ag_ysem,
    t_sem,
    p_sem,
    st_sem,
    row_send,
    row_recv,
    fwd_sem,
    go_sem,
):
    dp_count, tensor_count, rows, width, hidden = sizes
    per = dp_count // tensor_count
    tiles = hidden // 128
    cut = ((tiles * 5 + 8) // 9) * 128
    step_cols = 384
    seg = lax.axis_index("segment")
    i = lax.axis_index("dp")
    j = lax.axis_index("tensor")
    y = i // Z
    m = lax.rem(i, Z)
    across = (seg, (1 - y) * Z + m, j)
    side = (
        (seg, y * Z + lax.rem(m + Z - 1, Z), j),
        (seg, y * Z + lax.rem(m + 1, Z), j),
    )
    partner = (1 - seg, i, j)

    def at(offset):
        return lax.rem(m + offset + Z, Z)

    def dp_peer(r):
        return (seg, lax.rem(i + r, dp_count), j)

    def tensor_at(r):
        return lax.rem(j + r, tensor_count)

    def send(src, dst, send_sem, recv_sem, to):
        copy = pltpu.make_async_remote_copy(
            src_ref=src,
            dst_ref=dst,
            send_sem=send_sem,
            recv_sem=recv_sem,
            device_id=to,
            device_id_type=MESH,
        )
        copy.start()
        return copy

    def arrived(ref, sem):
        pltpu.make_async_copy(ref, ref, sem).wait()

    barrier = pltpu.get_barrier_semaphore()
    for r in range(1, dp_count):
        pl.semaphore_signal(barrier, inc=1, device_id=dp_peer(r), device_id_type=MESH)
    for r in range(1, tensor_count):
        pl.semaphore_signal(barrier, inc=1, device_id=(seg, i, tensor_at(r)), device_id_type=MESH)
    pl.semaphore_signal(barrier, inc=1, device_id=partner, device_id_type=MESH)
    loads = [
        pltpu.make_async_copy(src.at[0], dst, w_sem.at[n])
        for n, (src, dst) in enumerate(((wg_hbm, wg), (wu_hbm, wu), (wd_hbm, wd)))
    ]
    early = seg == 0
    late = seg == 1
    take_tokens = pltpu.make_async_copy(tokens_hbm, given, w_sem.at[3])
    take_cotangent = pltpu.make_async_copy(cotangent_hbm, given, w_sem.at[3])

    @pl.when(early)
    def _():
        take_tokens.start()
        take_tokens.wait()

    @pl.when(late)
    def _():
        take_cotangent.start()
        take_cotangent.wait()

    for load in loads:
        load.start()
    for b in range(dp_count):
        span = slice(b * width, (b + 1) * width)
        blocks[b] = given[:, span]
        gain_all[b : b + 1, :] = gains[:, span]
    tin[i] = blocks[i]
    with jax.named_scope("barrier"):
        pl.semaphore_wait(barrier, dp_count - 1 + tensor_count - 1 + 1)

    @pl.when(late)
    def _():
        pl.semaphore_wait(go_sem, 1)

    entry = []
    for r in range(1, dp_count):
        to = lax.rem(i + r, dp_count)
        entry.append(
            send(blocks.at[to], tin.at[i], in_sem.at[0, r], in_sem.at[1, r], (seg, to, j))
        )

    def write_inverse(source):
        def add(b, total):
            v = source[b].astype(F32)
            return total + v * v

        squares = lax.fori_loop(0, dp_count, add, jnp.zeros((rows, width), F32))
        mean = jnp.sum(squares, axis=1, keepdims=True) / (dp_count * width)
        inv[...] = jnp.broadcast_to(lax.rsqrt(mean + EPSILON), (rows, 128))

    def best_span(count, most):
        n = count // 128
        return max(k for k in range(1, n + 1) if n % k == 0 and k * 128 <= most) * 128

    @jax.named_scope("spread")
    def spread(x, weight, out, c0, count):
        span = best_span(count, 1792)

        def one(n, carry):
            c = pl.multiple_of(c0 + n * span, 128)
            v = jnp.dot(x, weight[:, pl.ds(c, span)], preferred_element_type=F32)
            out[:, :, :, pl.ds(c, span)] = v.astype(BF16).reshape(2, Z, rows, span)
            return carry

        if count == span:
            one(0, 0)
        else:
            lax.fori_loop(0, count // span, one, 0)

    @jax.named_scope("fold")
    def fold(left, weight, c0, count, first):
        span = best_span(count, 1152)

        def product(c):
            return lax.dot_general(
                rows_of(left[:, :, :, pl.ds(c, span)]),
                weight[:, pl.ds(c, span)],
                (((1,), (1,)), ((), ())),
                preferred_element_type=F32,
            )

        def one(n, carry):
            acc[...] += product(pl.multiple_of(c0 + n * span, 128))
            return carry

        if first:
            acc[...] = product(c0)
        lax.fori_loop(1 if first else 0, count // span, one, 0)

    class Ring:
        def __init__(self, own, land, pieces, sem):
            self.own, self.land, self.pieces, self.sem = own, land, pieces, sem
            self.last, self.sent = {}, []

        def cols(self, t, d, k):
            c0, w, _ = self.pieces[k]
            lead = (slice(None),) * (len(self.land.shape) - 3)
            return (t, d, *lead, pl.ds(c0, w))

        def push(self, t, d, k, src):
            copy = send(
                src,
                self.land.at[self.cols(t, d, k)],
                self.sem.at[0, t, d, k],
                self.sem.at[1, t, d, k],
                side[d],
            )
            self.last[t, d, k] = copy
            self.sent.append(copy)

        def dest(self, t, d):
            return at(t - 4 if d == 0 else 4 - t)

        def free(self, t, k):
            c0, w, anti = self.pieces[k]
            d = anti if t == 0 else 1 - anti
            self.push(t, d, k, self.own(self.dest(t, d), c0, w))

        def step(self, t):
            for k, (c0, w, anti) in enumerate(self.pieces):
                for d in (0, 1):
                    if t == 1 and d != anti:
                        continue
                    self.last[t - 1, d, k].wait_recv()
                    here = self.land.at[self.cols(t - 1, d, k)]
                    here[...] = here[...] + self.own(self.dest(t, d), c0, w)[...]
                    self.push(t, d, k, here)

        def finish(self, k):
            for d in (0, 1):
                self.last[3, d, k].wait_recv()

    def reduce_scatter(py, y0, wy, pz, z0, wz, by, ring_y, ring_z, z_out, z_fin, sem, ysem, fill_y, fill_z, aside):
        over_z = Ring(
            lambda dest, c0, w: pz.at[:, dest, :, pl.ds(z0 + c0, w)], ring_z, halves(wz // 128), sem.at[0]
        )
        over_y = Ring(lambda dest, c0, w: by.at[dest, :, pl.ds(c0, w)], ring_y, halves(wy // 128), sem.at[1])
        for k, (c0, w, _) in enumerate(over_z.pieces):
            fill_z(z0 + c0, w)
            over_z.free(0, k)
            over_z.free(1, k)
        for c0, w, _ in over_y.pieces:
            fill_y(y0 + c0, w)
        swaps = [
            send(
                py.at[1 - y, at(off), :, pl.ds(y0, wy)],
                by.at[at(off)],
                ysem.at[0, n],
                ysem.at[1, n],
                across,
            )
            for n, off in enumerate(ORDER)
        ]

        def pair(n):
            swaps[n].wait_recv()
            zd = at(ORDER[n])
            by[zd] = by[zd] + py[y, zd, :, pl.ds(y0, wy)]

        aside()

        def step_z(t):
            with jax.named_scope("z%d" % t):
                over_z.step(t)

        def step_y(t):
            with jax.named_scope("y%d" % t):
                over_y.step(t)

        step_z(1)
        pair(0)
        for k in (0, 1):
            over_y.free(0, k)
        step_z(2)
        pair(1)
        pair(2)
        for k in (0, 1):
            over_y.free(1, k)
        step_y(1)
        step_z(3)
        pair(3)
        pair(4)
        step_y(2)
        ends = []
        for k, (c0, w, _) in enumerate(over_z.pieces):
            with jax.named_scope("zf"):
                over_z.finish(k)
            cols = pl.ds(c0, w)
            z_out[:, cols] = (
                pz[1 - y, m, :, pl.ds(z0 + c0, w)].astype(F32)
                + ring_z[3, 0, 1 - y, :, cols].astype(F32)
                + ring_z[3, 1, 1 - y, :, cols].astype(F32)
            ).astype(BF16)
            ends.append(
                send(z_out.at[:, cols], z_fin.at[:, cols], ysem.at[0, Z + k], ysem.at[1, Z + k], across)
            )
        pair(5)
        pair(6)
        step_y(3)
        pair(7)
        with jax.named_scope("yf"):
            over_y.finish(0)
            over_y.finish(1)
        with jax.named_scope("last"):
            for copy in ends:
                copy.wait_recv()
        for copy in (*swaps, *over_z.sent, *over_y.sent, *ends):
            copy.wait_send()

    def y_total(by, ring_y, c, span):
        cols = pl.ds(c, span)
        return (
            by[m, :, cols].astype(F32) + ring_y[3, 0, :, cols].astype(F32) + ring_y[3, 1, :, cols].astype(F32)
        )

    def z_total(pz, z0, ring_z, z_fin, c, span):
        cols = pl.ds(c, span)
        return (
            pz[y, m, :, pl.ds(z0 + c, span)].astype(F32)
            + ring_z[3, 0, y, :, cols].astype(F32)
            + ring_z[3, 1, y, :, cols].astype(F32)
            + z_fin[:, cols].astype(F32)
        )

    @jax.named_scope("rs_dh")
    def scatter_hidden_grads(source, aside):
        x = rows_of(source[...])
        reduce_scatter(
            pd, 0, cut, pd, cut, hidden - cut, dh_y, dh_ring_y, dh_ring_z, dh_out, dh_fin, dh_sem, dh_ysem,
            lambda c, w: spread(x, wd, pd, c, w),
            lambda c, w: spread(x, wd, pd, c, w),
            aside,
        )
        dh_sum[:, pl.ds(0, cut)] = y_total(dh_y, dh_ring_y, 0, cut)
        dh_sum[:, pl.ds(cut, hidden - cut)] = z_total(pd, cut, dh_ring_z, dh_fin, 0, hidden - cut)

    def all_gather(a, a0, wa, b, b0, wb, sem, ysem, between):
        ca, cb = pl.ds(a0, wa), pl.ds(b0, wb)
        sent, over_a, over_b, cross = [], {}, {}, []

        def part(c0, w, t, d):
            if t < 3:
                return pl.ds(c0, w)
            h0, hw, _ = halves(w // 128)[d]
            return pl.ds(c0 + h0, hw)

        def push_a(t, d, origin):
            piece = a.at[y, origin, :, part(a0, wa, t, d)]
            over_a[t, d] = send(piece, piece, sem.at[0, 0, t, d], sem.at[0, 1, t, d], side[d])
            sent.append(over_a[t, d])

        def push_b(t, d, yy, origin):
            piece = b.at[yy, origin, :, part(b0, wb, t, d)]
            n = 1 if yy is y else 2
            over_b[n, t, d] = send(piece, piece, sem.at[n, 0, t, d], sem.at[n, 1, t, d], side[d])
            sent.append(over_b[n, t, d])

        def cross_a(origin):
            piece = a.at[y, origin, :, ca]
            n = len(cross)
            cross.append(send(piece, piece, ysem.at[0, n], ysem.at[1, n], across))

        def arrive_a(t):
            with jax.named_scope("A%d" % t):
                for d in (0, 1):
                    over_a[t - 1, d].wait_recv()
                    origin = at(t if d == 0 else -t)
                    if t < 4:
                        push_a(t, d, origin)
                        cross_a(origin)
                if t == 4:
                    cross_a(at(4))

        other = 1 - y

        def arrive_b(t, yy):
            n = 1 if yy is y else 2
            with jax.named_scope("%s%d" % (" bB"[n], t)):
                for d in (0, 1):
                    over_b[n, t - 1, d].wait_recv()
                    if t < 4:
                        push_b(t, d, yy, at(t if d == 0 else -t))

        mine = b.at[y, m, :, cb]
        first = send(mine, mine, ysem.at[0, Z], ysem.at[1, Z], across)
        push_a(0, 0, m)
        push_a(0, 1, m)
        push_b(0, 0, y, m)
        push_b(0, 1, y, m)
        cross_a(m)
        for t in (1, 2, 3, 4):
            arrive_a(t)
            if t == 1:
                with jax.named_scope("first"):
                    first.wait_recv()
                push_b(0, 0, other, m)
                push_b(0, 1, other, m)
            else:
                arrive_b(t - 1, other)
            if t < 4:
                arrive_b(t, y)
        with jax.named_scope("cross"):
            for copy in cross:
                copy.wait_recv()
        between()
        arrive_b(4, y)
        arrive_b(4, other)
        return [first, *sent, *cross]

    def drain(copies):
        for copy in copies:
            copy.wait_send()

    def row_block(turn, jd, q):
        if turn == 0 or per != 2:
            return per * jd + q
        return lax.rem(i + jd if q == 0 else i - 1 - jd + dp_count, dp_count)

    @jax.named_scope("tsum")
    def tensor_sum(turn):
        t_out[turn] = acc[...].reshape(dp_count, rows, width).astype(BF16)
        copies = {}
        for r in range(1, tensor_count):
            jd = tensor_at(r)
            for q in range(per):
                copies[r, q] = send(
                    t_out.at[turn, row_block(turn, jd, q)],
                    t_in.at[turn, r - 1, q],
                    t_sem.at[turn, 0, r, q],
                    t_sem.at[turn, 1, r, q],
                    (seg, i, jd),
                )
        totals = [t_out[turn, row_block(turn, j, q)].astype(F32) for q in range(per)]
        for r in range(1, tensor_count):
            for q in range(per):
                copies[r, q].wait_recv()
                totals[q] = totals[q] + t_in[turn, r - 1, q].astype(F32)
        return totals, list(copies.values())

    def to_partner_segment(src):
        copies = []
        for r in range(tensor_count):
            copies.append(
                send(
                    src,
                    pin.at[pl.ds(per * j, per)],
                    p_sem.at[0, r],
                    p_sem.at[1, r],
                    (1 - seg, i, tensor_at(r)),
                )
            )
        return copies

    @jax.named_scope("wait_seg")
    def from_partner_segment():
        for r in range(tensor_count):
            arrived(pin.at[pl.ds(0, per)], p_sem.at[1, r])

    @jax.named_scope("exchange")
    def exchange(land, kind):
        land[i] = pin[i]
        return [
            send(
                pin.at[lax.rem(i + r, dp_count)],
                land.at[i],
                row_send.at[kind, r],
                row_recv.at[kind, i],
                dp_peer(r),
            )
            for r in range(1, dp_count)
        ]

    @jax.named_scope("exchanged")
    def exchanged(land, kind):
        def one(r, carry):
            s = lax.rem(i + r, dp_count)
            arrived(land.at[s], row_recv.at[kind, s])
            return carry

        lax.fori_loop(1, dp_count, one, 0)

    def mine_too(q):
        return row_block(1, j, q) == i

    @jax.named_scope("to_rows")
    def to_rows(src, land):
        for r in range(tensor_count):
            for q in range(per):
                to = (seg, row_block(1, j, q), tensor_at(r))
                s = row_send.at[2, r * per + q]
                if r > 0:
                    send(src.at[q], land.at[i], s, row_recv.at[2, i], to)
                    continue

                @pl.when(mine_too(q))
                def _():
                    land[i] = src[q]

                @pl.when(jnp.logical_not(mine_too(q)))
                def _():
                    send(src.at[q], land.at[i], s, row_recv.at[2, i], to)

    def drain_rows(src):
        for r in range(tensor_count):
            for q in range(per):
                if r > 0:
                    arrived(src.at[q], row_send.at[2, r * per + q])
                    continue

                @pl.when(jnp.logical_not(mine_too(q)))
                def _():
                    arrived(src.at[q], row_send.at[2, r * per + q])

    @jax.named_scope("rows_wait")
    def rows_arrived(land):
        own = mine_too(0)
        for q in range(1, per):
            own = jnp.logical_or(own, mine_too(q))

        def one(r, carry):
            s = lax.rem(i + r, dp_count)
            arrived(land.at[s], row_recv.at[2, s])
            return carry

        lax.fori_loop(1, dp_count, one, 0)

        @pl.when(jnp.logical_not(own))
        def _():
            arrived(land.at[i], row_recv.at[2, i])

    here = pl.ds(per * j, per)
    gain_row = gain_all[pl.ds(i, 1), :]

    with jax.named_scope("entry_wait"):
        for copy in entry:
            copy.wait_recv()

    def scale(source):
        xg[...] = (rows_of(source[...]).astype(F32) * gain_row).astype(BF16)

    @pl.when(early)
    def _():
        pl.semaphore_signal(go_sem, inc=1, device_id=partner, device_id_type=MESH)
        scale(tin)

    @pl.when(late)
    def _():
        loads[2].wait()
        pl.semaphore_wait(go_sem, 1)
        scatter_hidden_grads(tin, lambda: None)
        from_partner_segment()
        scale(pin)

    loads[0].wait()
    loads[1].wait()

    def hand_early_rows():
        @pl.when(late)
        def _():
            exchange(rows_early, 0)

    def drain_exchange(land, kind):
        for r in range(1, dp_count):
            arrived(land.at[0], row_send.at[kind, r])

    with jax.named_scope("rs_gu"):
        reduce_scatter(
            pg, 0, hidden, pu, 0, hidden, gu_y, gu_ring_y, gu_ring_z, gu_out, gu_fin, gu_sem, gu_ysem,
            lambda c, w: spread(xg[...], wg, pg, c, w),
            lambda c, w: spread(xg[...], wu, pu, c, w),
            hand_early_rows,
        )

    @pl.when(early)
    def _():
        write_inverse(blocks)

    @pl.when(late)
    def _():
        exchanged(rows_early, 0)
        write_inverse(rows_early)

    def activate(n, carry):
        c = pl.multiple_of(n * step_cols, 128)
        cols = pl.ds(c, step_cols)
        factor = inv[:, 0:1]
        gate = factor * y_total(gu_y, gu_ring_y, c, step_cols)
        up = factor * z_total(pu, 0, gu_ring_z, gu_fin, c, step_cols)
        stash_g[:, cols] = gate.astype(BF16)
        stash_u[:, cols] = up.astype(BF16)
        hid[y, m, :, cols] = (gate * jax.nn.sigmoid(gate) * up).astype(BF16)
        return carry

    lax.fori_loop(0, hidden // step_cols, activate, 0)

    def put_rows(out, source):
        for b in range(dp_count):
            out[0, :, b * width : (b + 1) * width] = source[b]

    def write_hidden_grads():
        def one(n, carry):
            c = pl.multiple_of(n * step_cols, 128)
            cols = pl.ds(c, step_cols)
            g = stash_g[:, cols].astype(F32)
            u = stash_u[:, cols].astype(F32)
            d = dh_sum[:, cols]
            s = jax.nn.sigmoid(g)
            dg[y, m, :, cols] = (d * u * s * (1.0 + g * (1.0 - s))).astype(BF16)
            du[y, m, :, cols] = (d * g * s).astype(BF16)
            return carry

        lax.fori_loop(0, hidden // step_cols, one, 0)

    a_cols = cut
    b_cols = hidden - cut

    @jax.named_scope("ag_hid")
    def gather_hidden():
        sent = all_gather(
            hid, 0, a_cols, hid, a_cols, b_cols, ag_sem.at[0], ag_ysem.at[0],
            lambda: fold(hid, wd, 0, a_cols, True),
        )
        fold(hid, wd, a_cols, b_cols, False)
        return sent

    @jax.named_scope("ag_dgu")
    def gather_hidden_grads():
        sent = all_gather(
            dg, 0, hidden, du, 0, hidden, ag_sem.at[1], ag_ysem.at[1],
            lambda: fold(dg, wg, 0, hidden, True),
        )
        fold(du, wu, 0, hidden, False)
        return sent

    @pl.when(early)
    def _():
        loads[2].wait()
        pl.semaphore_signal(go_sem, inc=1, device_id=partner, device_id_type=MESH)
        gathers = gather_hidden()
        totals, sums = tensor_sum(0)
        for q in range(per):
            made[0, q] = (tin[row_block(0, j, q)].astype(F32) + totals[q]).astype(BF16)
        handed = to_partner_segment(made.at[0])
        drain(gathers)
        drain(sums)
        drain(handed)
        from_partner_segment()
        scatter_hidden_grads(pin, lambda: exchange(rows_back, 1))
        write_hidden_grads()
        gathers = gather_hidden_grads()
        exchanged(rows_back, 1)
        back = send(rows_back, rows_back, fwd_sem.at[0, 1], fwd_sem.at[1, 1], partner)
        totals, sums = tensor_sum(1)
        for q in range(per):
            made[1, q] = totals[q].astype(BF16)
        to_rows(made.at[1], rows_last)
        arrived(rows_early, fwd_sem.at[1, 0])
        put_rows(acts, rows_early)
        rows_arrived(rows_last)
        factor = inv[:, 0:1]
        project = jnp.zeros((rows, width), F32)
        for b in range(dp_count):
            weighted = rows_last[b].astype(F32) * gain_all[b : b + 1, :]
            project = project + weighted * (blocks[b].astype(F32) * factor)
        mean = jnp.sum(project, axis=1, keepdims=True) / (dp_count * width)
        for b in range(dp_count):
            weighted = rows_last[b].astype(F32) * gain_all[b : b + 1, :]
            unit = blocks[b].astype(F32) * factor
            grads[0, :, b * width : (b + 1) * width] = (rows_back[b].astype(F32) + factor * (weighted - unit * mean)).astype(BF16)
        back.wait_send()
        drain(gathers)
        drain(sums)
        drain_rows(made.at[1])
        drain_exchange(rows_back, 1)

    @pl.when(late)
    def _():
        write_hidden_grads()
        gathers = gather_hidden_grads()
        totals, sums = tensor_sum(0)
        weighted = jnp.concatenate(totals, axis=0) * gain_row
        e = rows_of(pin[here]).astype(F32)
        count = per * rows
        both = jnp.concatenate([weighted * e, e * e], axis=0)
        st_out[...] = jnp.zeros_like(st_out)
        st_out[:, pl.ds(0, 2 * count)] = lax.dot_general(
            jnp.ones((8, width), F32),
            both,
            (((1,), (1,)), ((), ())),
            preferred_element_type=F32,
            precision=lax.Precision.HIGHEST,
        )
        stats = [
            send(st_out, st_in.at[r], st_sem.at[0, r], st_sem.at[1, r], dp_peer(r)) for r in range(1, dp_count)
        ]
        tally = st_out[...]
        for r in range(1, dp_count):
            with jax.named_scope("st"):
                stats[r - 1].wait_recv()
            tally = tally + st_in[r]
        turned = tally.T
        dot_e = turned[0:count, 0:1] / (dp_count * width)
        squares = turned[count : 2 * count, 0:1] / (dp_count * width)
        factor = lax.rsqrt(squares + EPSILON)
        c = rows_of(tin[here]).astype(F32)
        d_in = c + factor * (weighted - e * factor * (factor * dot_e))
        made[0] = d_in.astype(BF16).reshape(per, rows, width)
        handed = to_partner_segment(made.at[0])
        drain(gathers)
        drain(sums)
        drain(stats)
        gathers = gather_hidden()
        totals, sums = tensor_sum(1)
        for q in range(per):
            made[1, q] = (pin[row_block(1, j, q)].astype(F32) + totals[q]).astype(BF16)
        to_rows(made.at[1], rows_last)
        ahead = send(rows_early, rows_early, fwd_sem.at[0, 0], fwd_sem.at[1, 0], partner)
        arrived(rows_back, fwd_sem.at[1, 1])
        put_rows(grads, rows_back)
        rows_arrived(rows_last)
        put_rows(acts, rows_last)
        ahead.wait_send()
        drain(gathers)
        drain(sums)
        drain(handed)
        drain_rows(made.at[1])
        drain_exchange(rows_early, 0)

    for copy in entry:
        copy.wait_send()


def solution(mesh):
    dp_count, tensor_count = mesh.shape["dp"], mesh.shape["tensor"]

    def body(tokens, cotangent, gains, w_gate, w_up, w_down):
        rows, model = tokens.shape
        _, width, hidden = w_gate.shape
        per = dp_count // tensor_count
        tiles = hidden // 128
        cut = ((tiles * 5 + 8) // 9) * 128
        rest = hidden - cut
        def buf(*shape, dtype=BF16):
            return pltpu.VMEM(shape, dtype)

        block = (dp_count, rows, width)
        wide = (2, Z, rows, hidden)
        dma = pltpu.SemaphoreType.DMA
        scratch = [
            buf(rows, model),
            buf(*block),
            buf(dp_count, width, dtype=F32),
            buf(width, hidden),
            buf(width, hidden),
            buf(width, hidden),
            buf(*block),
            buf(*block),
            buf(dp_count * rows, width),
            buf(*wide),
            buf(*wide),
            buf(*wide),
            buf(Z, rows, hidden),
            buf(4, 2, rows, hidden),
            buf(4, 2, 2, rows, hidden),
            buf(rows, hidden),
            buf(rows, hidden),
            buf(Z, rows, cut),
            buf(4, 2, rows, cut),
            buf(4, 2, 2, rows, rest),
            buf(rows, rest),
            buf(rows, rest),
            buf(rows, hidden),
            buf(rows, hidden),
            buf(rows, hidden, dtype=F32),
            buf(*wide),
            buf(*wide),
            buf(*wide),
            buf(dp_count * rows, width, dtype=F32),
            buf(2, *block),
            buf(2, tensor_count - 1, per, rows, width),
            buf(2, per, rows, width),
            buf(8, 128, dtype=F32),
            buf(dp_count, 8, 128, dtype=F32),
            buf(*block),
            buf(*block),
            buf(*block),
            buf(rows, 128, dtype=F32),
            dma((4,)),
            dma((2, dp_count)),
            dma((2, 2, 4, 2, 2)),
            dma((2, Z + 2)),
            dma((2, 2, 4, 2, 2)),
            dma((2, Z + 2)),
            dma((2, 3, 2, 4, 2)),
            dma((2, 2, Z + 1)),
            dma((2, 2, tensor_count, per)),
            dma((2, tensor_count)),
            dma((2, dp_count)),
            dma((3, dp_count)),
            dma((3, dp_count)),
            dma((2, 2)),
            pltpu.SemaphoreType.REGULAR,
        ]
        vmem = pl.BlockSpec(memory_space=pltpu.VMEM)
        hbm = pl.BlockSpec(memory_space=pl.ANY)
        acts, grads = pl.pallas_call(
            functools.partial(kernel, (dp_count, tensor_count, rows, width, hidden)),
            out_shape=[jax.ShapeDtypeStruct((1, rows, model), BF16)] * 2,
            in_specs=[hbm, hbm, vmem, hbm, hbm, hbm],
            out_specs=[vmem, vmem],
            scratch_shapes=scratch,
            compiler_params=pltpu.CompilerParams(collective_id=0, has_side_effects=True),
        )(tokens, cotangent, gains, w_gate, w_up, w_down)

        return acts, grads

    in_specs = (
        P("dp", None),
        P("dp", None),
        P("segment", None),
        P("segment", "dp", "tensor"),
        P("segment", "dp", "tensor"),
        P("segment", "dp", "tensor"),
    )
    out_specs = (P("segment", "dp", None), P("segment", "dp", None))
    return jax.shard_map(body, mesh=mesh, in_specs=in_specs, out_specs=out_specs, check_vma=False)
```

```python
import functools

import jax
import jax.numpy as jnp
from jax import lax
from jax.experimental import pallas as pl
from jax.experimental.pallas import tpu as pltpu
from jax.sharding import PartitionSpec as P

EPSILON = 1e-06
MESH = pl.DeviceIdType.MESH
F32 = jnp.float32
BF16 = jnp.bfloat16
GU_FAR, DH_FAR, HID_FAR, DGU_FAR = False, False, False, False
Z = 8
ORDER = (4, 3, -3, 2, -2, 1, -1, 0)


def halves(tiles):
    first = (tiles + 1) // 2
    return ((0, first * 128, 0), (first * 128, (tiles - first) * 128, 1))


def rows_of(block):
    return block.reshape(-1, block.shape[-1])


def kernel(
    sizes,
    tokens_hbm,
    cotangent_hbm,
    gains,
    wg_hbm,
    wu_hbm,
    wd_hbm,
    acts,
    grads,
    given,
    blocks,
    gain_all,
    wg,
    wu,
    wd,
    tin,
    pin,
    xg,
    pg,
    pu,
    pd,
    gu_y,
    gu_ring_y,
    gu_ring_z,
    gu_out,
    gu_fin,
    dh_y,
    dh_ring_y,
    dh_ring_z,
    dh_out,
    dh_fin,
    stash_g,
    stash_u,
    dh_sum,
    hid,
    dg,
    du,
    acc,
    t_out,
    t_in,
    made,
    st_out,
    st_in,
    rows_early,
    rows_back,
    rows_last,
    inv,
    w_sem,
    in_sem,
    gu_sem,
    gu_ysem,
    dh_sem,
    dh_ysem,
    ag_sem,
    ag_ysem,
    t_sem,
    p_sem,
    st_sem,
    row_sem,
    fwd_sem,
    go_sem,
):
    dp_count, tensor_count, rows, width, hidden = sizes
    per = dp_count // tensor_count
    tiles = hidden // 128
    cut = ((tiles * 5 + 8) // 9) * 128
    step_cols = 384
    seg = lax.axis_index("segment")
    i = lax.axis_index("dp")
    j = lax.axis_index("tensor")
    y = i // Z
    m = lax.rem(i, Z)
    across = (seg, (1 - y) * Z + m, j)
    partner = (1 - seg, i, j)

    def beside(d, steps):
        return (seg, y * Z + lax.rem(m + (Z - steps if d == 0 else steps), Z), j)

    others = pl.ds(0, dp_count - 1)

    def at(offset):
        return lax.rem(m + offset + Z, Z)

    def dp_peer(r):
        return (seg, lax.rem(i + r, dp_count), j)

    def tensor_at(r):
        return lax.rem(j + r, tensor_count)

    def send(src, dst, send_sem, recv_sem, to):
        copy = pltpu.make_async_remote_copy(
            src_ref=src,
            dst_ref=dst,
            send_sem=send_sem,
            recv_sem=recv_sem,
            device_id=to,
            device_id_type=MESH,
        )
        copy.start()
        return copy

    def arrived(ref, sem):
        pltpu.make_async_copy(ref, ref, sem).wait()

    barrier = pltpu.get_barrier_semaphore()
    for r in range(1, dp_count):
        pl.semaphore_signal(barrier, inc=1, device_id=dp_peer(r), device_id_type=MESH)
    for r in range(1, tensor_count):
        pl.semaphore_signal(barrier, inc=1, device_id=(seg, i, tensor_at(r)), device_id_type=MESH)
    pl.semaphore_signal(barrier, inc=1, device_id=partner, device_id_type=MESH)
    loads = [
        pltpu.make_async_copy(src.at[0], dst, w_sem.at[n])
        for n, (src, dst) in enumerate(((wg_hbm, wg), (wu_hbm, wu), (wd_hbm, wd)))
    ]
    early = seg == 0
    late = seg == 1
    take_tokens = pltpu.make_async_copy(tokens_hbm, given, w_sem.at[3])
    take_cotangent = pltpu.make_async_copy(cotangent_hbm, given, w_sem.at[3])

    @pl.when(early)
    def _():
        take_tokens.start()
        take_tokens.wait()

    @pl.when(late)
    def _():
        take_cotangent.start()
        take_cotangent.wait()

    for load in loads:
        load.start()
    for b in range(dp_count):
        span = slice(b * width, (b + 1) * width)
        blocks[b] = given[:, span]
        gain_all[b : b + 1, :] = gains[:, span]
    tin[i] = blocks[i]
    with jax.named_scope("barrier"):
        pl.semaphore_wait(barrier, dp_count - 1 + tensor_count - 1 + 1)

    @pl.when(late)
    def _():
        pl.semaphore_wait(go_sem, 1)

    for r in range(1, dp_count):
        to = lax.rem(i + r, dp_count)
        send(blocks.at[to], tin.at[i], in_sem.at[0], in_sem.at[1], (seg, to, j))

    def write_inverse(source):
        def add(b, total):
            v = source[b].astype(F32)
            return total + v * v

        squares = lax.fori_loop(0, dp_count, add, jnp.zeros((rows, width), F32))
        mean = jnp.sum(squares, axis=1, keepdims=True) / (dp_count * width)
        inv[...] = jnp.broadcast_to(lax.rsqrt(mean + EPSILON), (rows, 128))

    def best_span(count, most):
        n = count // 128
        return max(k for k in range(1, n + 1) if n % k == 0 and k * 128 <= most) * 128

    @jax.named_scope("spread")
    def spread(x, weight, out, c0, count):
        span = best_span(count, 1792)

        def one(n, carry):
            c = pl.multiple_of(c0 + n * span, 128)
            v = jnp.dot(x, weight[:, pl.ds(c, span)], preferred_element_type=F32)
            out[:, :, :, pl.ds(c, span)] = v.astype(BF16).reshape(2, Z, rows, span)
            return carry

        if count == span:
            one(0, 0)
        else:
            lax.fori_loop(0, count // span, one, 0)

    @jax.named_scope("fold")
    def fold(left, weight, c0, count, first):
        span = best_span(count, 1152)

        def product(c):
            return lax.dot_general(
                rows_of(left[:, :, :, pl.ds(c, span)]),
                weight[:, pl.ds(c, span)],
                (((1,), (1,)), ((), ())),
                preferred_element_type=F32,
            )

        def one(n, carry):
            acc[...] += product(pl.multiple_of(c0 + n * span, 128))
            return carry

        if first:
            acc[...] = product(c0)
        lax.fori_loop(1 if first else 0, count // span, one, 0)

    class Ring:
        def __init__(self, own, land, pieces, out_sem, sem, far):
            self.own, self.land, self.pieces, self.out_sem, self.sem, self.far = own, land, pieces, out_sem, sem, far
            self.last = {}

        def cols(self, t, d, k):
            c0, w, _ = self.pieces[k]
            lead = (slice(None),) * (len(self.land.shape) - 3)
            return (t, d, *lead, pl.ds(c0, w))

        def push(self, t, d, k, src):
            copy = send(
                src,
                self.land.at[self.cols(t, d, k)],
                self.out_sem,
                self.sem.at[t, d, k],
                beside(d, 2 if self.far and t in (0, 2) else 1),
            )
            self.last[t, d, k] = copy

        def dest(self, t, d):
            return at(t - 4 if d == 0 else 4 - t)

        def free(self, distance, k):
            c0, w, anti = self.pieces[k]
            t = 4 - distance
            for d in (0, 1):
                if t == 0 and d != anti or t == 1 and d == anti and not self.far:
                    continue
                if t == 2 or t == 3 and not self.far:
                    continue
                self.push(t, d, k, self.own(self.dest(t, d), c0, w))

        def step(self, t):
            if self.far:
                self.join(t)
                return
            for k, (c0, w, anti) in enumerate(self.pieces):
                for d in (0, 1):
                    if t == 1 and d != anti:
                        continue
                    self.last[t - 1, d, k].wait_recv()
                    here = self.land.at[self.cols(t - 1, d, k)]
                    here[...] = here[...] + self.own(self.dest(t, d), c0, w)[...]
                    self.push(t, d, k, here)

        def join(self, t):
            if t != 2:
                return
            for k, (c0, w, anti) in enumerate(self.pieces):
                for d in (0, 1):
                    self.last[1, d, k].wait_recv()
                    here = self.land.at[self.cols(1, d, k)]
                    total = here[...].astype(F32) + self.own(self.dest(2, d), c0, w)[...].astype(F32)
                    if d == anti:
                        self.last[0, d, k].wait_recv()
                        total = total + self.land[self.cols(0, d, k)].astype(F32)
                    here[...] = total.astype(BF16)
                    self.push(2, d, k, here)

        def finish(self, k):
            for d in (0, 1):
                self.last[3, d, k].wait_recv()
                if self.far:
                    self.last[2, d, k].wait_recv()

    def ring_total(land, far, *index):
        total = land[(3, 0, *index)].astype(F32) + land[(3, 1, *index)].astype(F32)
        if far:
            total = total + land[(2, 0, *index)].astype(F32) + land[(2, 1, *index)].astype(F32)
        return total

    def reduce_scatter(py, y0, wy, pz, z0, wz, by, ring_y, ring_z, z_out, z_fin, sem, ysem, fill_y, fill_z, aside, far):
        over_z = Ring(
            lambda dest, c0, w: pz.at[:, dest, :, pl.ds(z0 + c0, w)], ring_z, halves(wz // 128), ysem.at[1], sem.at[0], far
        )
        over_y = Ring(
            lambda dest, c0, w: by.at[dest, :, pl.ds(c0, w)], ring_y, halves(wy // 128), ysem.at[2], sem.at[1], far
        )
        for k, (c0, w, _) in enumerate(over_z.pieces):
            fill_z(z0 + c0, w)
            for distance in (4, 3, 1):
                over_z.free(distance, k)
        for c0, w, _ in over_y.pieces:
            fill_y(y0 + c0, w)
        swaps = [
            send(
                py.at[1 - y, at(off), :, pl.ds(y0, wy)],
                by.at[at(off)],
                ysem.at[0],
                ysem.at[5 + n],
                across,
            )
            for n, off in enumerate(ORDER)
        ]

        def pair(n):
            swaps[n].wait_recv()
            zd = at(ORDER[n])
            by[zd] = by[zd] + py[y, zd, :, pl.ds(y0, wy)]

        aside()

        def step_z(t):
            with jax.named_scope("z%d" % t):
                over_z.step(t)

        def step_y(t):
            with jax.named_scope("y%d" % t):
                over_y.step(t)

        step_z(1)
        pair(0)
        for k in (0, 1):
            over_y.free(4, k)
        step_z(2)
        pair(1)
        pair(2)
        for k in (0, 1):
            over_y.free(3, k)
        step_y(1)
        step_z(3)
        pair(3)
        pair(4)
        step_y(2)
        for k, (c0, w, _) in enumerate(over_z.pieces):
            with jax.named_scope("zf"):
                over_z.finish(k)
            cols = pl.ds(c0, w)
            z_out[:, cols] = (
                pz[1 - y, m, :, pl.ds(z0 + c0, w)].astype(F32)
                + ring_total(ring_z, far, 1 - y, slice(None), cols)
            ).astype(BF16)
            send(z_out.at[:, cols], z_fin.at[:, cols], ysem.at[3], ysem.at[4], across)
        pair(5)
        pair(6)
        for k in (0, 1):
            over_y.free(1, k)
        step_y(3)
        pair(7)
        with jax.named_scope("yf"):
            over_y.finish(0)
            over_y.finish(1)
        with jax.named_scope("last"):
            arrived(z_fin, ysem.at[4])
        arrived(by, ysem.at[0])
        arrived(pz.at[:, pl.ds(0, 7), :, pl.ds(z0, wz)], ysem.at[1])
        arrived(by.at[pl.ds(0, 7)], ysem.at[2])
        arrived(z_out, ysem.at[3])

    def y_total(by, ring_y, c, span, far):
        cols = pl.ds(c, span)
        return by[m, :, cols].astype(F32) + ring_total(ring_y, far, slice(None), cols)

    def z_total(pz, z0, ring_z, z_fin, c, span, far):
        cols = pl.ds(c, span)
        return (
            pz[y, m, :, pl.ds(z0 + c, span)].astype(F32)
            + ring_total(ring_z, far, y, slice(None), cols)
            + z_fin[:, cols].astype(F32)
        )

    @jax.named_scope("rs_dh")
    def scatter_hidden_grads(source, aside):
        x = rows_of(source[...])
        reduce_scatter(
            pd, 0, cut, pd, cut, hidden - cut, dh_y, dh_ring_y, dh_ring_z, dh_out, dh_fin, dh_sem, dh_ysem,
            lambda c, w: spread(x, wd, pd, c, w),
            lambda c, w: spread(x, wd, pd, c, w),
            aside,
            DH_FAR,
        )
        dh_sum[:, pl.ds(0, cut)] = y_total(dh_y, dh_ring_y, 0, cut, DH_FAR)
        dh_sum[:, pl.ds(cut, hidden - cut)] = z_total(pd, cut, dh_ring_z, dh_fin, 0, hidden - cut, DH_FAR)

    def gather_steps(a, a0, wa, b, b0, wb, sem, ysem, far):
        ca, cb = pl.ds(a0, wa), pl.ds(b0, wb)
        over_a, over_b = {}, {}

        def part(c0, w, t, d):
            if t < 3:
                return pl.ds(c0, w)
            h0, hw, _ = halves(w // 128)[d]
            return pl.ds(c0 + h0, hw)

        def push_a(t, d, origin):
            piece = a.at[y, origin, :, part(a0, wa, t, d)]
            over_a[t, d] = send(piece, piece, ysem.at[0], sem.at[0, t, d], beside(d, 2 if far and t in (1, 3) else 1))

        def push_b(t, d, yy, origin):
            piece = b.at[yy, origin, :, part(b0, wb, t, d)]
            n = 1 if yy is y else 2
            over_b[n, t, d] = send(piece, piece, ysem.at[1], sem.at[n, t, d], beside(d, 2 if far and t in (1, 3) else 1))

        def forwards(t):
            if far:
                return (2, 3) if t == 2 else ()
            return (t,) if t < 4 else ()

        def cross_a(origin):
            piece = a.at[y, origin, :, ca]
            send(piece, piece, ysem.at[2], ysem.at[3], across)

        def arrive_a(t):
            with jax.named_scope("A%d" % t):
                for d in (0, 1):
                    over_a[t - 1, d].wait_recv()
                    origin = at(t if d == 0 else -t)
                    for later in forwards(t):
                        push_a(later, d, origin)
                    if t < 4:
                        cross_a(origin)
                if t == 4:
                    cross_a(at(4))

        other = 1 - y

        def arrive_b(t, yy):
            n = 1 if yy is y else 2
            with jax.named_scope("%s%d" % (" bB"[n], t)):
                for d in (0, 1):
                    over_b[n, t - 1, d].wait_recv()
                    for later in forwards(t):
                        push_b(later, d, yy, at(t if d == 0 else -t))

        mine = b.at[y, m, :, cb]
        first = send(mine, mine, ysem.at[4], ysem.at[5], across)
        starts = (1, 0) if far else (0,)
        for t in starts:
            for d in (0, 1):
                push_a(t, d, m)
        for t in starts:
            for d in (0, 1):
                push_b(t, d, y, m)
        cross_a(m)
        yield 0
        for t in (1, 2, 3, 4):
            arrive_a(t)
            if t == 1:
                with jax.named_scope("first"):
                    first.wait_recv()
                for start in starts:
                    for d in (0, 1):
                        push_b(start, d, other, m)
            else:
                arrive_b(t - 1, other)
            if t < 4:
                arrive_b(t, y)
                yield t
        with jax.named_scope("cross"):
            arrived(a.at[0, :, :, ca], ysem.at[3])
        yield 4
        arrive_b(4, y)
        arrive_b(4, other)
        yield 5

    def advance(steps, to):
        while next(steps) != to:
            pass

    def gathered(a, a0, wa, b, b0, wb, ysem):
        ca, cb = pl.ds(a0, wa), pl.ds(b0, wb)
        arrived(a.at[0, pl.ds(0, 7), :, ca], ysem.at[0])
        arrived(b.at[:, pl.ds(0, 7), :, cb], ysem.at[1])
        arrived(a.at[0, :, :, ca], ysem.at[2])
        arrived(b.at[0, 0, :, cb], ysem.at[4])

    def row_block(turn, jd, q):
        if turn == 0 or per != 2:
            return per * jd + q
        return lax.rem(i + jd if q == 0 else i - 1 - jd + dp_count, dp_count)

    def tensor_send(turn):
        t_out[turn] = acc[...].reshape(dp_count, rows, width).astype(BF16)
        for r in range(1, tensor_count):
            jd = tensor_at(r)
            for q in range(per):
                send(
                    t_out.at[turn, row_block(turn, jd, q)],
                    t_in.at[turn, r - 1, q],
                    t_sem.at[turn, 0],
                    t_sem.at[turn, 1],
                    (seg, i, jd),
                )

    @jax.named_scope("tsum")
    def tensor_sum(turn):
        arrived(t_in.at[turn], t_sem.at[turn, 1])
        totals = [t_out[turn, row_block(turn, j, q)].astype(F32) for q in range(per)]
        for r in range(1, tensor_count):
            for q in range(per):
                totals[q] = totals[q] + t_in[turn, r - 1, q].astype(F32)
        return totals

    def to_partner_segment(src):
        for r in range(tensor_count):
            send(src, pin.at[pl.ds(per * j, per)], p_sem.at[0], p_sem.at[1], (1 - seg, i, tensor_at(r)))

    @jax.named_scope("wait_seg")
    def from_partner_segment():
        arrived(pin, p_sem.at[1])

    @jax.named_scope("exchange")
    def exchange(land, kind):
        land[i] = pin[i]
        for r in range(1, dp_count):
            send(pin.at[lax.rem(i + r, dp_count)], land.at[i], row_sem.at[kind, 0], row_sem.at[kind, 1], dp_peer(r))

    @jax.named_scope("exchanged")
    def exchanged(land, kind):
        arrived(land.at[others], row_sem.at[kind, 1])

    def mine_too(q):
        return row_block(1, j, q) == i

    @jax.named_scope("to_rows")
    def to_rows(src, land):
        for r in range(tensor_count):
            for q in range(per):
                to = (seg, row_block(1, j, q), tensor_at(r))
                out, into = row_sem.at[2, 0], row_sem.at[2, 1]
                if r > 0:
                    send(src.at[q], land.at[i], out, into, to)
                    continue

                @pl.when(mine_too(q))
                def _():
                    land[i] = src[q]

                @pl.when(jnp.logical_not(mine_too(q)))
                def _():
                    send(src.at[q], land.at[i], out, into, to)

    def rows_done(land, n):
        own = mine_too(0)
        for q in range(1, per):
            own = jnp.logical_or(own, mine_too(q))

        @pl.when(own)
        def _():
            arrived(land.at[others], row_sem.at[2, n])

        @pl.when(jnp.logical_not(own))
        def _():
            arrived(land, row_sem.at[2, n])

    @jax.named_scope("rows_wait")
    def rows_arrived(land):
        rows_done(land, 1)

    here = pl.ds(per * j, per)
    gain_row = gain_all[pl.ds(i, 1), :]

    with jax.named_scope("entry_wait"):
        arrived(tin.at[others], in_sem.at[1])

    def scale(source):
        xg[...] = (rows_of(source[...]).astype(F32) * gain_row).astype(BF16)

    @pl.when(early)
    def _():
        pl.semaphore_signal(go_sem, inc=1, device_id=partner, device_id_type=MESH)
        scale(tin)

    @pl.when(late)
    def _():
        loads[2].wait()
        pl.semaphore_wait(go_sem, 1)
        scatter_hidden_grads(tin, lambda: None)
        from_partner_segment()
        scale(pin)

    loads[0].wait()
    loads[1].wait()

    def hand_early_rows():
        @pl.when(late)
        def _():
            exchange(rows_early, 0)

    def drain_exchange(land, kind):
        arrived(land.at[others], row_sem.at[kind, 0])

    with jax.named_scope("rs_gu"):
        reduce_scatter(
            pg, 0, hidden, pu, 0, hidden, gu_y, gu_ring_y, gu_ring_z, gu_out, gu_fin, gu_sem, gu_ysem,
            lambda c, w: spread(xg[...], wg, pg, c, w),
            lambda c, w: spread(xg[...], wu, pu, c, w),
            hand_early_rows,
            GU_FAR,
        )

    @pl.when(early)
    def _():
        write_inverse(blocks)

    @pl.when(late)
    def _():
        exchanged(rows_early, 0)
        write_inverse(rows_early)

    def activate(n, carry):
        c = pl.multiple_of(n * step_cols, 128)
        cols = pl.ds(c, step_cols)
        factor = inv[:, 0:1]
        gate = factor * y_total(gu_y, gu_ring_y, c, step_cols, GU_FAR)
        up = factor * z_total(pu, 0, gu_ring_z, gu_fin, c, step_cols, GU_FAR)
        stash_g[:, cols] = gate.astype(BF16)
        stash_u[:, cols] = up.astype(BF16)
        hid[y, m, :, cols] = (gate * jax.nn.sigmoid(gate) * up).astype(BF16)
        return carry

    lax.fori_loop(0, hidden // step_cols, activate, 0)

    def put_rows(out, source):
        for b in range(dp_count):
            out[0, :, b * width : (b + 1) * width] = source[b]

    def write_hidden_grads():
        def one(n, carry):
            c = pl.multiple_of(n * step_cols, 128)
            cols = pl.ds(c, step_cols)
            g = stash_g[:, cols].astype(F32)
            u = stash_u[:, cols].astype(F32)
            d = dh_sum[:, cols]
            s = jax.nn.sigmoid(g)
            dg[y, m, :, cols] = (d * u * s * (1.0 + g * (1.0 - s))).astype(BF16)
            du[y, m, :, cols] = (d * g * s).astype(BF16)
            return carry

        lax.fori_loop(0, hidden // step_cols, one, 0)

    a_cols = cut
    b_cols = hidden - cut

    hid_args = (hid, 0, a_cols, hid, a_cols, b_cols)
    dgu_args = (dg, 0, hidden, du, 0, hidden)

    def start_hidden():
        return gather_steps(*hid_args, ag_sem.at[0], ag_ysem.at[0], HID_FAR)

    @jax.named_scope("ag_hid")
    def finish_hidden(steps):
        advance(steps, 4)
        fold(hid, wd, 0, a_cols, True)
        advance(steps, 5)
        fold(hid, wd, a_cols, b_cols, False)

    @jax.named_scope("ag_dgu")
    def gather_hidden_grads(beside_fold):
        steps = gather_steps(*dgu_args, ag_sem.at[1], ag_ysem.at[1], DGU_FAR)
        advance(steps, 4)
        beside_fold()
        fold(dg, wg, 0, hidden, True)
        advance(steps, 5)
        fold(du, wu, 0, hidden, False)

    @pl.when(early)
    def _():
        loads[2].wait()
        pl.semaphore_signal(go_sem, inc=1, device_id=partner, device_id_type=MESH)
        finish_hidden(start_hidden())
        tensor_send(0)
        totals = tensor_sum(0)
        for q in range(per):
            made[0, q] = (tin[row_block(0, j, q)].astype(F32) + totals[q]).astype(BF16)
        to_partner_segment(made.at[0])
        from_partner_segment()
        scatter_hidden_grads(pin, lambda: exchange(rows_back, 1))
        write_hidden_grads()
        gather_hidden_grads(lambda: None)
        tensor_send(1)
        exchanged(rows_back, 1)
        back = send(rows_back, rows_back, fwd_sem.at[0, 1], fwd_sem.at[1, 1], partner)
        totals = tensor_sum(1)
        for q in range(per):
            made[1, q] = totals[q].astype(BF16)
        to_rows(made.at[1], rows_last)
        arrived(rows_early, fwd_sem.at[1, 0])
        put_rows(acts, rows_early)
        rows_arrived(rows_last)
        factor = inv[:, 0:1]
        project = jnp.zeros((rows, width), F32)
        for b in range(dp_count):
            weighted = rows_last[b].astype(F32) * gain_all[b : b + 1, :]
            project = project + weighted * (blocks[b].astype(F32) * factor)
        mean = jnp.sum(project, axis=1, keepdims=True) / (dp_count * width)
        for b in range(dp_count):
            weighted = rows_last[b].astype(F32) * gain_all[b : b + 1, :]
            unit = blocks[b].astype(F32) * factor
            grads[0, :, b * width : (b + 1) * width] = (rows_back[b].astype(F32) + factor * (weighted - unit * mean)).astype(BF16)
        back.wait_send()
        drain_exchange(rows_back, 1)

    @pl.when(late)
    def _():
        write_hidden_grads()
        steps = start_hidden()
        gather_hidden_grads(lambda: advance(steps, 0))
        tensor_send(0)
        advance(steps, 1)
        totals = tensor_sum(0)
        weighted = jnp.concatenate(totals, axis=0) * gain_row
        e = rows_of(pin[here]).astype(F32)
        count = per * rows
        both = jnp.concatenate([weighted * e, e * e], axis=0)
        st_out[...] = jnp.zeros_like(st_out)
        st_out[:, pl.ds(0, 2 * count)] = lax.dot_general(
            jnp.ones((8, width), F32),
            both,
            (((1,), (1,)), ((), ())),
            preferred_element_type=F32,
            precision=lax.Precision.HIGHEST,
        )
        for r in range(1, dp_count):
            send(st_out, st_in.at[r], st_sem.at[0], st_sem.at[1], dp_peer(r))
        advance(steps, 2)
        with jax.named_scope("st"):
            arrived(st_in.at[pl.ds(1, dp_count - 1)], st_sem.at[1])
        tally = st_out[...]
        for r in range(1, dp_count):
            tally = tally + st_in[r]
        turned = tally.T
        dot_e = turned[0:count, 0:1] / (dp_count * width)
        squares = turned[count : 2 * count, 0:1] / (dp_count * width)
        factor = lax.rsqrt(squares + EPSILON)
        c = rows_of(tin[here]).astype(F32)
        d_in = c + factor * (weighted - e * factor * (factor * dot_e))
        made[0] = d_in.astype(BF16).reshape(per, rows, width)
        to_partner_segment(made.at[0])
        finish_hidden(steps)
        tensor_send(1)
        totals = tensor_sum(1)
        for q in range(per):
            made[1, q] = (pin[row_block(1, j, q)].astype(F32) + totals[q]).astype(BF16)
        to_rows(made.at[1], rows_last)
        ahead = send(rows_early, rows_early, fwd_sem.at[0, 0], fwd_sem.at[1, 0], partner)
        arrived(rows_back, fwd_sem.at[1, 1])
        put_rows(grads, rows_back)
        rows_arrived(rows_last)
        put_rows(acts, rows_last)
        ahead.wait_send()
        drain_exchange(rows_early, 0)
        arrived(st_in.at[pl.ds(1, dp_count - 1)], st_sem.at[0])

    gathered(*hid_args, ag_ysem.at[0])
    gathered(*dgu_args, ag_ysem.at[1])
    for turn in (0, 1):
        arrived(t_in.at[turn], t_sem.at[turn, 0])
    arrived(pin, p_sem.at[0])
    rows_done(rows_last, 0)
    arrived(blocks.at[others], in_sem.at[0])


def solution(mesh):
    dp_count, tensor_count = mesh.shape["dp"], mesh.shape["tensor"]

    def body(tokens, cotangent, gains, w_gate, w_up, w_down):
        rows, model = tokens.shape
        _, width, hidden = w_gate.shape
        per = dp_count // tensor_count
        tiles = hidden // 128
        cut = ((tiles * 5 + 8) // 9) * 128
        rest = hidden - cut
        def buf(*shape, dtype=BF16):
            return pltpu.VMEM(shape, dtype)

        block = (dp_count, rows, width)
        wide = (2, Z, rows, hidden)
        dma = pltpu.SemaphoreType.DMA
        scratch = [
            buf(rows, model),
            buf(*block),
            buf(dp_count, width, dtype=F32),
            buf(width, hidden),
            buf(width, hidden),
            buf(width, hidden),
            buf(*block),
            buf(*block),
            buf(dp_count * rows, width),
            buf(*wide),
            buf(*wide),
            buf(*wide),
            buf(Z, rows, hidden),
            buf(4, 2, rows, hidden),
            buf(4, 2, 2, rows, hidden),
            buf(rows, hidden),
            buf(rows, hidden),
            buf(Z, rows, cut),
            buf(4, 2, rows, cut),
            buf(4, 2, 2, rows, rest),
            buf(rows, rest),
            buf(rows, rest),
            buf(rows, hidden),
            buf(rows, hidden),
            buf(rows, hidden, dtype=F32),
            buf(*wide),
            buf(*wide),
            buf(*wide),
            buf(dp_count * rows, width, dtype=F32),
            buf(2, *block),
            buf(2, tensor_count - 1, per, rows, width),
            buf(2, per, rows, width),
            buf(8, 128, dtype=F32),
            buf(dp_count, 8, 128, dtype=F32),
            buf(*block),
            buf(*block),
            buf(*block),
            buf(rows, 128, dtype=F32),
            dma((4,)),
            dma((2,)),
            dma((2, 4, 2, 2)),
            dma((5 + Z,)),
            dma((2, 4, 2, 2)),
            dma((5 + Z,)),
            dma((2, 3, 4, 2)),
            dma((2, 6)),
            dma((2, 2)),
            dma((2,)),
            dma((2,)),
            dma((3, 2)),
            dma((2, 2)),
            pltpu.SemaphoreType.REGULAR,
        ]
        vmem = pl.BlockSpec(memory_space=pltpu.VMEM)
        hbm = pl.BlockSpec(memory_space=pl.ANY)
        acts, grads = pl.pallas_call(
            functools.partial(kernel, (dp_count, tensor_count, rows, width, hidden)),
            out_shape=[jax.ShapeDtypeStruct((1, rows, model), BF16)] * 2,
            in_specs=[hbm, hbm, vmem, hbm, hbm, hbm],
            out_specs=[vmem, vmem],
            scratch_shapes=scratch,
            compiler_params=pltpu.CompilerParams(collective_id=0, has_side_effects=True),
        )(tokens, cotangent, gains, w_gate, w_up, w_down)

        return acts, grads

    in_specs = (
        P("dp", None),
        P("dp", None),
        P("segment", None),
        P("segment", "dp", "tensor"),
        P("segment", "dp", "tensor"),
        P("segment", "dp", "tensor"),
    )
    out_specs = (P("segment", "dp", None), P("segment", "dp", None))
    return jax.shard_map(body, mesh=mesh, in_specs=in_specs, out_specs=out_specs, check_vma=False)
```

```python
import functools

import jax
import jax.numpy as jnp
from jax import lax
from jax.experimental import pallas as pl
from jax.experimental.pallas import tpu as pltpu
from jax.sharding import PartitionSpec as P

EPSILON = 1e-06
MESH = pl.DeviceIdType.MESH
F32 = jnp.float32
BF16 = jnp.bfloat16
GU_FAR, DH_FAR = False, False
Z = 8
ORDER = (4, 3, -3, 2, -2, 1, -1, 0)


def halves(tiles):
    first = (tiles + 1) // 2
    return ((0, first * 128, 0), (first * 128, (tiles - first) * 128, 1))


def rows_of(block):
    return block.reshape(-1, block.shape[-1])


def kernel(
    sizes,
    tokens_hbm,
    cotangent_hbm,
    gains,
    wg_hbm,
    wu_hbm,
    wd_hbm,
    out_early,
    out_last,
    out_back,
    given,
    blocks,
    gain_all,
    wg,
    wu,
    wd,
    tin,
    pin,
    xg,
    pg,
    pu,
    pd,
    gu_y,
    gu_ring_y,
    gu_ring_z,
    gu_out,
    gu_fin,
    dh_y,
    dh_ring_y,
    dh_ring_z,
    dh_out,
    dh_fin,
    stash_g,
    stash_u,
    dh_sum,
    hid,
    dg,
    du,
    acc,
    t_out,
    t_in,
    made,
    st_out,
    st_in,
    rows_early,
    rows_back,
    rows_last,
    inv,
    w_sem,
    in_sem,
    gu_sem,
    gu_ysem,
    dh_sem,
    dh_ysem,
    ag_sem,
    ag_ysem,
    t_sem,
    p_sem,
    st_sem,
    row_sem,
    fwd_sem,
    go_sem,
):
    dp_count, tensor_count, rows, width, hidden = sizes
    per = dp_count // tensor_count
    tiles = hidden // 128
    cut = ((tiles * 5 + 8) // 9) * 128
    step_cols = 384
    seg = lax.axis_index("segment")
    i = lax.axis_index("dp")
    j = lax.axis_index("tensor")
    y = i // Z
    m = lax.rem(i, Z)
    across = (seg, (1 - y) * Z + m, j)
    partner = (1 - seg, i, j)

    def beside(d, steps):
        return (seg, y * Z + lax.rem(m + (Z - steps if d == 0 else steps), Z), j)

    others = pl.ds(0, dp_count - 1)

    def at(offset):
        return lax.rem(m + offset + Z, Z)

    def dp_peer(r):
        return (seg, lax.rem(i + r, dp_count), j)

    def tensor_at(r):
        return lax.rem(j + r, tensor_count)

    def send(src, dst, send_sem, recv_sem, to):
        copy = pltpu.make_async_remote_copy(
            src_ref=src,
            dst_ref=dst,
            send_sem=send_sem,
            recv_sem=recv_sem,
            device_id=to,
            device_id_type=MESH,
        )
        copy.start()
        return copy

    def arrived(ref, sem):
        pltpu.make_async_copy(ref, ref, sem).wait()

    barrier = pltpu.get_barrier_semaphore()
    for r in range(1, dp_count):
        pl.semaphore_signal(barrier, inc=1, device_id=dp_peer(r), device_id_type=MESH)
    for r in range(1, tensor_count):
        pl.semaphore_signal(barrier, inc=1, device_id=(seg, i, tensor_at(r)), device_id_type=MESH)
    pl.semaphore_signal(barrier, inc=1, device_id=partner, device_id_type=MESH)
    loads = [
        pltpu.make_async_copy(src.at[0], dst, w_sem.at[n])
        for n, (src, dst) in enumerate(((wg_hbm, wg), (wu_hbm, wu), (wd_hbm, wd)))
    ]
    early = seg == 0
    late = seg == 1
    take_tokens = pltpu.make_async_copy(tokens_hbm, given, w_sem.at[3])
    take_cotangent = pltpu.make_async_copy(cotangent_hbm, given, w_sem.at[3])

    @pl.when(early)
    def _():
        take_tokens.start()
        take_tokens.wait()

    @pl.when(late)
    def _():
        take_cotangent.start()
        take_cotangent.wait()

    for load in loads:
        load.start()
    for b in range(dp_count):
        span = slice(b * width, (b + 1) * width)
        blocks[b] = given[:, span]
        gain_all[b : b + 1, :] = gains[:, span]
    tin[i] = blocks[i]
    with jax.named_scope("barrier"):
        pl.semaphore_wait(barrier, dp_count - 1 + tensor_count - 1 + 1)

    @pl.when(late)
    def _():
        pl.semaphore_wait(go_sem, 1)

    for r in range(1, dp_count):
        to = lax.rem(i + r, dp_count)
        send(blocks.at[to], tin.at[i], in_sem.at[0], in_sem.at[1], (seg, to, j))

    def write_inverse(source):
        def add(b, total):
            v = source[b].astype(F32)
            return total + v * v

        squares = lax.fori_loop(0, dp_count, add, jnp.zeros((rows, width), F32))
        mean = jnp.sum(squares, axis=1, keepdims=True) / (dp_count * width)
        inv[...] = jnp.broadcast_to(lax.rsqrt(mean + EPSILON), (rows, 128))

    def best_span(count, most):
        n = count // 128
        return max(k for k in range(1, n + 1) if n % k == 0 and k * 128 <= most) * 128

    @jax.named_scope("spread")
    def spread(x, weight, out, c0, count):
        span = best_span(count, 1792)

        def one(n, carry):
            c = pl.multiple_of(c0 + n * span, 128)
            v = jnp.dot(x, weight[:, pl.ds(c, span)], preferred_element_type=F32)
            out[:, :, :, pl.ds(c, span)] = v.astype(BF16).reshape(2, Z, rows, span)
            return carry

        if count == span:
            one(0, 0)
        else:
            lax.fori_loop(0, count // span, one, 0)

    @jax.named_scope("fold")
    def fold(left, weight, c0, count, first):
        span = best_span(count, 1152)

        def product(c):
            return lax.dot_general(
                rows_of(left[:, :, :, pl.ds(c, span)]),
                weight[:, pl.ds(c, span)],
                (((1,), (1,)), ((), ())),
                preferred_element_type=F32,
            )

        def one(n, carry):
            acc[...] += product(pl.multiple_of(c0 + n * span, 128))
            return carry

        if first:
            acc[...] = product(c0)
        lax.fori_loop(1 if first else 0, count // span, one, 0)

    class Ring:
        def __init__(self, own, land, pieces, out_sem, sem, far):
            self.own, self.land, self.pieces, self.out_sem, self.sem, self.far = own, land, pieces, out_sem, sem, far
            self.last = {}

        def cols(self, t, d, k):
            c0, w, _ = self.pieces[k]
            lead = (slice(None),) * (len(self.land.shape) - 3)
            return (t, d, *lead, pl.ds(c0, w))

        def push(self, t, d, k, src):
            copy = send(
                src,
                self.land.at[self.cols(t, d, k)],
                self.out_sem,
                self.sem.at[t, d, k],
                beside(d, 2 if self.far and t in (0, 2) else 1),
            )
            self.last[t, d, k] = copy

        def dest(self, t, d):
            return at(t - 4 if d == 0 else 4 - t)

        def free(self, distance, k):
            c0, w, anti = self.pieces[k]
            t = 4 - distance
            for d in (0, 1):
                if t == 0 and d != anti or t == 1 and d == anti and not self.far:
                    continue
                if t == 2 or t == 3 and not self.far:
                    continue
                self.push(t, d, k, self.own(self.dest(t, d), c0, w))

        def step(self, t):
            if self.far:
                self.join(t)
                return
            for k, (c0, w, anti) in enumerate(self.pieces):
                for d in (0, 1):
                    if t == 1 and d != anti:
                        continue
                    self.last[t - 1, d, k].wait_recv()
                    here = self.land.at[self.cols(t - 1, d, k)]
                    here[...] = here[...] + self.own(self.dest(t, d), c0, w)[...]
                    self.push(t, d, k, here)

        def join(self, t):
            if t != 2:
                return
            for k, (c0, w, anti) in enumerate(self.pieces):
                for d in (0, 1):
                    self.last[1, d, k].wait_recv()
                    here = self.land.at[self.cols(1, d, k)]
                    total = here[...].astype(F32) + self.own(self.dest(2, d), c0, w)[...].astype(F32)
                    if d == anti:
                        self.last[0, d, k].wait_recv()
                        total = total + self.land[self.cols(0, d, k)].astype(F32)
                    here[...] = total.astype(BF16)
                    self.push(2, d, k, here)

        def finish(self, k):
            for d in (0, 1):
                self.last[3, d, k].wait_recv()
                if self.far:
                    self.last[2, d, k].wait_recv()

    def ring_total(land, far, *index):
        total = land[(3, 0, *index)].astype(F32) + land[(3, 1, *index)].astype(F32)
        if far:
            total = total + land[(2, 0, *index)].astype(F32) + land[(2, 1, *index)].astype(F32)
        return total

    def reduce_scatter(py, y0, wy, pz, z0, wz, by, ring_y, ring_z, z_out, z_fin, sem, ysem, fill_y, fill_z, aside, far):
        over_z = Ring(
            lambda dest, c0, w: pz.at[:, dest, :, pl.ds(z0 + c0, w)], ring_z, halves(wz // 128), ysem.at[1], sem.at[0], far
        )
        over_y = Ring(
            lambda dest, c0, w: by.at[dest, :, pl.ds(c0, w)], ring_y, halves(wy // 128), ysem.at[2], sem.at[1], far
        )
        for k, (c0, w, _) in enumerate(over_z.pieces):
            fill_z(z0 + c0, w)
            for distance in (4, 3, 1):
                over_z.free(distance, k)
        for c0, w, _ in over_y.pieces:
            fill_y(y0 + c0, w)
        swaps = [
            send(
                py.at[1 - y, at(off), :, pl.ds(y0, wy)],
                by.at[at(off)],
                ysem.at[0],
                ysem.at[5 + n],
                across,
            )
            for n, off in enumerate(ORDER)
        ]

        def pair(n):
            swaps[n].wait_recv()
            zd = at(ORDER[n])
            by[zd] = by[zd] + py[y, zd, :, pl.ds(y0, wy)]

        aside()

        def step_z(t):
            with jax.named_scope("z%d" % t):
                over_z.step(t)

        def step_y(t):
            with jax.named_scope("y%d" % t):
                over_y.step(t)

        step_z(1)
        pair(0)
        for k in (0, 1):
            over_y.free(4, k)
        step_z(2)
        pair(1)
        pair(2)
        for k in (0, 1):
            over_y.free(3, k)
        step_y(1)
        step_z(3)
        pair(3)
        pair(4)
        step_y(2)
        for k, (c0, w, _) in enumerate(over_z.pieces):
            with jax.named_scope("zf"):
                over_z.finish(k)
            cols = pl.ds(c0, w)
            z_out[:, cols] = (
                pz[1 - y, m, :, pl.ds(z0 + c0, w)].astype(F32)
                + ring_total(ring_z, far, 1 - y, slice(None), cols)
            ).astype(BF16)
            send(z_out.at[:, cols], z_fin.at[:, cols], ysem.at[3], ysem.at[4], across)
        pair(5)
        pair(6)
        for k in (0, 1):
            over_y.free(1, k)
        step_y(3)
        pair(7)
        with jax.named_scope("yf"):
            over_y.finish(0)
            over_y.finish(1)
        with jax.named_scope("last"):
            arrived(z_fin, ysem.at[4])
        arrived(by, ysem.at[0])
        arrived(pz.at[:, pl.ds(0, 7), :, pl.ds(z0, wz)], ysem.at[1])
        arrived(by.at[pl.ds(0, 7)], ysem.at[2])
        arrived(z_out, ysem.at[3])

    def y_total(by, ring_y, c, span, far):
        cols = pl.ds(c, span)
        return by[m, :, cols].astype(F32) + ring_total(ring_y, far, slice(None), cols)

    def z_total(pz, z0, ring_z, z_fin, c, span, far):
        cols = pl.ds(c, span)
        return (
            pz[y, m, :, pl.ds(z0 + c, span)].astype(F32)
            + ring_total(ring_z, far, y, slice(None), cols)
            + z_fin[:, cols].astype(F32)
        )

    @jax.named_scope("rs_dh")
    def scatter_hidden_grads(source, aside):
        x = rows_of(source[...])
        reduce_scatter(
            pd, 0, cut, pd, cut, hidden - cut, dh_y, dh_ring_y, dh_ring_z, dh_out, dh_fin, dh_sem, dh_ysem,
            lambda c, w: spread(x, wd, pd, c, w),
            lambda c, w: spread(x, wd, pd, c, w),
            aside,
            DH_FAR,
        )
        dh_sum[:, pl.ds(0, cut)] = y_total(dh_y, dh_ring_y, 0, cut, DH_FAR)
        dh_sum[:, pl.ds(cut, hidden - cut)] = z_total(pd, cut, dh_ring_z, dh_fin, 0, hidden - cut, DH_FAR)

    def gather_steps(a, a0, wa, b, b0, wb, sem, ysem):
        ca, cb = pl.ds(a0, wa), pl.ds(b0, wb)
        over_a, over_b = {}, {}
        other = 1 - y

        def part(c0, w, k):
            h0, hw, _ = halves(w // 128)[k]
            return pl.ds(c0 + h0, hw)

        def push_a(t, d, k, origin):
            piece = a.at[y, origin, :, part(a0, wa, k)]
            over_a[t, d, k] = send(piece, piece, ysem.at[0], sem.at[0, t, d, k], beside(d, 1))

        def push_b(t, d, k, yy, origin):
            piece = b.at[yy, origin, :, part(b0, wb, k)]
            n = 1 if yy is y else 2
            over_b[n, t, d, k] = send(piece, piece, ysem.at[1], sem.at[n, t, d, k], beside(d, 1))

        def cross_a(origin, k):
            piece = a.at[y, origin, :, part(a0, wa, k)]
            send(piece, piece, ysem.at[2], ysem.at[3], across)

        def arrive(t, over, push, *cross):
            for k in (0, 1):
                for d in (0, 1):
                    if t == 4 and d != k:
                        continue
                    over[t - 1, d, k].wait_recv()
                    origin = at(t if d == 0 else -t)
                    if t < 3 or t == 3 and d == k:
                        push(t, d, k, origin)
                    for to in cross:
                        to(origin, k)

        def arrive_a(t):
            with jax.named_scope("A%d" % t):
                arrive(t, over_a, push_a, cross_a)

        def arrive_b(t, yy):
            n = 1 if yy is y else 2
            with jax.named_scope("%s%d" % (" bB"[n], t)):
                arrive(
                    t,
                    {key[1:]: copy for key, copy in over_b.items() if key[0] == n},
                    lambda t, d, k, origin: push_b(t, d, k, yy, origin),
                )

        mine = b.at[y, m, :, cb]
        first = send(mine, mine, ysem.at[4], ysem.at[5], across)
        for k in (0, 1):
            for d in (0, 1):
                push_a(0, d, k, m)
        for k in (0, 1):
            for d in (0, 1):
                push_b(0, d, k, y, m)
        for k in (0, 1):
            cross_a(m, k)
        yield 0
        for t in (1, 2, 3, 4):
            arrive_a(t)
            if t == 1:
                with jax.named_scope("first"):
                    first.wait_recv()
                for k in (0, 1):
                    for d in (0, 1):
                        push_b(0, d, k, other, m)
            else:
                arrive_b(t - 1, other)
            if t < 4:
                arrive_b(t, y)
                yield t
        with jax.named_scope("cross"):
            arrived(a.at[0, :, :, ca], ysem.at[3])
        yield 4
        arrive_b(4, y)
        arrive_b(4, other)
        yield 5

    def advance(steps, to):
        while next(steps) != to:
            pass

    def gathered(a, a0, wa, b, b0, wb, ysem):
        ca, cb = pl.ds(a0, wa), pl.ds(b0, wb)
        arrived(a.at[0, pl.ds(0, 7), :, ca], ysem.at[0])
        arrived(b.at[:, pl.ds(0, 7), :, cb], ysem.at[1])
        arrived(a.at[0, :, :, ca], ysem.at[2])
        arrived(b.at[0, 0, :, cb], ysem.at[4])

    def row_block(turn, jd, q):
        if turn == 0 or per != 2:
            return per * jd + q
        return lax.rem(i + jd if q == 0 else i - 1 - jd + dp_count, dp_count)

    def tensor_send(turn):
        t_out[turn] = acc[...].reshape(dp_count, rows, width).astype(BF16)
        for r in range(1, tensor_count):
            jd = tensor_at(r)
            for q in range(per):
                send(
                    t_out.at[turn, row_block(turn, jd, q)],
                    t_in.at[turn, r - 1, q],
                    t_sem.at[turn, 0],
                    t_sem.at[turn, 1],
                    (seg, i, jd),
                )

    @jax.named_scope("tsum")
    def tensor_sum(turn):
        arrived(t_in.at[turn], t_sem.at[turn, 1])
        totals = [t_out[turn, row_block(turn, j, q)].astype(F32) for q in range(per)]
        for r in range(1, tensor_count):
            for q in range(per):
                totals[q] = totals[q] + t_in[turn, r - 1, q].astype(F32)
        return totals

    def to_partner_segment(src):
        for r in range(tensor_count):
            send(src, pin.at[pl.ds(per * j, per)], p_sem.at[0], p_sem.at[1], (1 - seg, i, tensor_at(r)))

    @jax.named_scope("wait_seg")
    def from_partner_segment():
        arrived(pin, p_sem.at[1])

    @jax.named_scope("exchange")
    def exchange(land, kind):
        land[i] = pin[i]
        for r in range(1, dp_count):
            send(pin.at[lax.rem(i + r, dp_count)], land.at[i], row_sem.at[kind, 0], row_sem.at[kind, 1], dp_peer(r))

    @jax.named_scope("exchanged")
    def exchanged(land, kind):
        arrived(land.at[others], row_sem.at[kind, 1])

    def mine_too(q):
        return row_block(1, j, q) == i

    @jax.named_scope("to_rows")
    def to_rows(src, land):
        for r in range(tensor_count):
            for q in range(per):
                to = (seg, row_block(1, j, q), tensor_at(r))
                out, into = row_sem.at[2, 0], row_sem.at[2, 1]
                if r > 0:
                    send(src.at[q], land.at[i], out, into, to)
                    continue

                @pl.when(mine_too(q))
                def _():
                    land[i] = src[q]

                @pl.when(jnp.logical_not(mine_too(q)))
                def _():
                    send(src.at[q], land.at[i], out, into, to)

    def rows_done(land, n):
        own = mine_too(0)
        for q in range(1, per):
            own = jnp.logical_or(own, mine_too(q))

        @pl.when(own)
        def _():
            arrived(land.at[others], row_sem.at[2, n])

        @pl.when(jnp.logical_not(own))
        def _():
            arrived(land, row_sem.at[2, n])

    @jax.named_scope("rows_wait")
    def rows_arrived(land):
        rows_done(land, 1)

    here = pl.ds(per * j, per)
    gain_row = gain_all[pl.ds(i, 1), :]

    with jax.named_scope("entry_wait"):
        arrived(tin.at[others], in_sem.at[1])

    def scale(source):
        xg[...] = (rows_of(source[...]).astype(F32) * gain_row).astype(BF16)

    @pl.when(early)
    def _():
        pl.semaphore_signal(go_sem, inc=1, device_id=partner, device_id_type=MESH)
        scale(tin)

    @pl.when(late)
    def _():
        loads[2].wait()
        pl.semaphore_wait(go_sem, 1)
        scatter_hidden_grads(tin, lambda: None)
        from_partner_segment()
        scale(pin)

    loads[0].wait()
    loads[1].wait()

    def hand_early_rows():
        @pl.when(late)
        def _():
            exchange(rows_early, 0)

    def drain_exchange(land, kind):
        arrived(land.at[others], row_sem.at[kind, 0])

    with jax.named_scope("rs_gu"):
        reduce_scatter(
            pg, 0, hidden, pu, 0, hidden, gu_y, gu_ring_y, gu_ring_z, gu_out, gu_fin, gu_sem, gu_ysem,
            lambda c, w: spread(xg[...], wg, pg, c, w),
            lambda c, w: spread(xg[...], wu, pu, c, w),
            hand_early_rows,
            GU_FAR,
        )

    @pl.when(early)
    def _():
        write_inverse(blocks)

    @pl.when(late)
    def _():
        exchanged(rows_early, 0)
        write_inverse(rows_early)

    def activate(n, carry):
        c = pl.multiple_of(n * step_cols, 128)
        cols = pl.ds(c, step_cols)
        factor = inv[:, 0:1]
        gate = factor * y_total(gu_y, gu_ring_y, c, step_cols, GU_FAR)
        up = factor * z_total(pu, 0, gu_ring_z, gu_fin, c, step_cols, GU_FAR)
        stash_g[:, cols] = gate.astype(BF16)
        stash_u[:, cols] = up.astype(BF16)
        hid[y, m, :, cols] = (gate * jax.nn.sigmoid(gate) * up).astype(BF16)
        return carry

    lax.fori_loop(0, hidden // step_cols, activate, 0)

    def put_rows(out, source):
        for b in range(dp_count):
            out[0, :, b * width : (b + 1) * width] = source[b]

    def write_hidden_grads():
        def one(n, carry):
            c = pl.multiple_of(n * step_cols, 128)
            cols = pl.ds(c, step_cols)
            g = stash_g[:, cols].astype(F32)
            u = stash_u[:, cols].astype(F32)
            d = dh_sum[:, cols]
            s = jax.nn.sigmoid(g)
            dg[y, m, :, cols] = (d * u * s * (1.0 + g * (1.0 - s))).astype(BF16)
            du[y, m, :, cols] = (d * g * s).astype(BF16)
            return carry

        lax.fori_loop(0, hidden // step_cols, one, 0)

    a_cols = cut
    b_cols = hidden - cut

    hid_args = (hid, 0, a_cols, hid, a_cols, b_cols)
    dgu_args = (dg, 0, hidden, du, 0, hidden)

    def start_hidden():
        return gather_steps(*hid_args, ag_sem.at[0], ag_ysem.at[0])

    @jax.named_scope("ag_hid")
    def finish_hidden(steps):
        advance(steps, 4)
        fold(hid, wd, 0, a_cols, True)
        advance(steps, 5)
        fold(hid, wd, a_cols, b_cols, False)

    @jax.named_scope("ag_dgu")
    def gather_hidden_grads(beside_fold):
        steps = gather_steps(*dgu_args, ag_sem.at[1], ag_ysem.at[1])
        advance(steps, 4)
        beside_fold()
        fold(dg, wg, 0, hidden, True)
        advance(steps, 5)
        fold(du, wu, 0, hidden, False)

    @pl.when(early)
    def _():
        loads[2].wait()
        pl.semaphore_signal(go_sem, inc=1, device_id=partner, device_id_type=MESH)
        finish_hidden(start_hidden())
        tensor_send(0)
        totals = tensor_sum(0)
        for q in range(per):
            made[0, q] = (tin[row_block(0, j, q)].astype(F32) + totals[q]).astype(BF16)
        to_partner_segment(made.at[0])
        from_partner_segment()
        scatter_hidden_grads(pin, lambda: None)
        write_hidden_grads()
        gather_hidden_grads(lambda: None)
        pl.semaphore_signal(go_sem, inc=1, device_id=partner, device_id_type=MESH)
        tensor_send(1)
        exchange(rows_back, 1)
        totals = tensor_sum(1)
        for q in range(per):
            made[1, q] = totals[q].astype(BF16)
        to_rows(made.at[1], rows_last)
        exchanged(rows_back, 1)
        back = send(rows_back, rows_back, fwd_sem.at[0, 1], fwd_sem.at[1, 1], partner)
        arrived(rows_early, fwd_sem.at[1, 0])
        put_rows(out_early, rows_early)
        put_rows(out_back, rows_back)
        rows_arrived(rows_last)
        factor = inv[:, 0:1]
        project = jnp.zeros((rows, width), F32)
        for b in range(dp_count):
            weighted = rows_last[b].astype(F32) * gain_all[b : b + 1, :]
            project = project + weighted * (blocks[b].astype(F32) * factor)
        mean = jnp.sum(project, axis=1, keepdims=True) / (dp_count * width)
        for b in range(dp_count):
            weighted = rows_last[b].astype(F32) * gain_all[b : b + 1, :]
            unit = blocks[b].astype(F32) * factor
            out_last[0, :, b * width : (b + 1) * width] = (rows_back[b].astype(F32) + factor * (weighted - unit * mean)).astype(BF16)
        back.wait_send()
        drain_exchange(rows_back, 1)

    @pl.when(late)
    def _():
        write_hidden_grads()
        steps = start_hidden()
        gather_hidden_grads(lambda: advance(steps, 0))
        tensor_send(0)
        advance(steps, 1)
        totals = tensor_sum(0)
        weighted = jnp.concatenate(totals, axis=0) * gain_row
        e = rows_of(pin[here]).astype(F32)
        count = per * rows
        both = jnp.concatenate([weighted * e, e * e], axis=0)
        st_out[...] = jnp.zeros_like(st_out)
        st_out[:, pl.ds(0, 2 * count)] = lax.dot_general(
            jnp.ones((8, width), F32),
            both,
            (((1,), (1,)), ((), ())),
            preferred_element_type=F32,
            precision=lax.Precision.HIGHEST,
        )
        for r in range(1, dp_count):
            send(st_out, st_in.at[r], st_sem.at[0], st_sem.at[1], dp_peer(r))
        advance(steps, 2)
        with jax.named_scope("st"):
            arrived(st_in.at[pl.ds(1, dp_count - 1)], st_sem.at[1])
        tally = st_out[...]
        for r in range(1, dp_count):
            tally = tally + st_in[r]
        turned = tally.T
        dot_e = turned[0:count, 0:1] / (dp_count * width)
        squares = turned[count : 2 * count, 0:1] / (dp_count * width)
        factor = lax.rsqrt(squares + EPSILON)
        c = rows_of(tin[here]).astype(F32)
        d_in = c + factor * (weighted - e * factor * (factor * dot_e))
        made[0] = d_in.astype(BF16).reshape(per, rows, width)
        to_partner_segment(made.at[0])
        finish_hidden(steps)
        tensor_send(1)
        totals = tensor_sum(1)
        for q in range(per):
            made[1, q] = (pin[row_block(1, j, q)].astype(F32) + totals[q]).astype(BF16)
        pl.semaphore_wait(go_sem, 1)
        to_rows(made.at[1], rows_last)
        ahead = send(rows_early, rows_early, fwd_sem.at[0, 0], fwd_sem.at[1, 0], partner)
        arrived(rows_back, fwd_sem.at[1, 1])
        put_rows(out_early, rows_early)
        put_rows(out_back, rows_back)
        rows_arrived(rows_last)
        put_rows(out_last, rows_last)
        ahead.wait_send()
        drain_exchange(rows_early, 0)
        arrived(st_in.at[pl.ds(1, dp_count - 1)], st_sem.at[0])

    gathered(*hid_args, ag_ysem.at[0])
    gathered(*dgu_args, ag_ysem.at[1])
    for turn in (0, 1):
        arrived(t_in.at[turn], t_sem.at[turn, 0])
    arrived(pin, p_sem.at[0])
    rows_done(rows_last, 0)
    arrived(blocks.at[others], in_sem.at[0])


def solution(mesh):
    dp_count, tensor_count = mesh.shape["dp"], mesh.shape["tensor"]

    def body(tokens, cotangent, gains, w_gate, w_up, w_down):
        rows, model = tokens.shape
        _, width, hidden = w_gate.shape
        per = dp_count // tensor_count
        tiles = hidden // 128
        cut = ((tiles * 5 + 8) // 9) * 128
        rest = hidden - cut
        def buf(*shape, dtype=BF16):
            return pltpu.VMEM(shape, dtype)

        block = (dp_count, rows, width)
        wide = (2, Z, rows, hidden)
        dma = pltpu.SemaphoreType.DMA
        scratch = [
            buf(rows, model),
            buf(*block),
            buf(dp_count, width, dtype=F32),
            buf(width, hidden),
            buf(width, hidden),
            buf(width, hidden),
            buf(*block),
            buf(*block),
            buf(dp_count * rows, width),
            buf(*wide),
            buf(*wide),
            buf(*wide),
            buf(Z, rows, hidden),
            buf(4, 2, rows, hidden),
            buf(4, 2, 2, rows, hidden),
            buf(rows, hidden),
            buf(rows, hidden),
            buf(Z, rows, cut),
            buf(4, 2, rows, cut),
            buf(4, 2, 2, rows, rest),
            buf(rows, rest),
            buf(rows, rest),
            buf(rows, hidden),
            buf(rows, hidden),
            buf(rows, hidden, dtype=F32),
            buf(*wide),
            buf(*wide),
            buf(*wide),
            buf(dp_count * rows, width, dtype=F32),
            buf(2, *block),
            buf(2, tensor_count - 1, per, rows, width),
            buf(2, per, rows, width),
            buf(8, 128, dtype=F32),
            buf(dp_count, 8, 128, dtype=F32),
            buf(*block),
            buf(*block),
            buf(*block),
            buf(rows, 128, dtype=F32),
            dma((4,)),
            dma((2,)),
            dma((2, 4, 2, 2)),
            dma((5 + Z,)),
            dma((2, 4, 2, 2)),
            dma((5 + Z,)),
            dma((2, 3, 4, 2, 2)),
            dma((2, 6)),
            dma((2, 2)),
            dma((2,)),
            dma((2,)),
            dma((3, 2)),
            dma((2, 2)),
            pltpu.SemaphoreType.REGULAR,
        ]
        vmem = pl.BlockSpec(memory_space=pltpu.VMEM)
        hbm = pl.BlockSpec(memory_space=pl.ANY)
        early_rows, last_rows, back_rows = pl.pallas_call(
            functools.partial(kernel, (dp_count, tensor_count, rows, width, hidden)),
            out_shape=[jax.ShapeDtypeStruct((1, rows, model), BF16)] * 3,
            in_specs=[hbm, hbm, vmem, hbm, hbm, hbm],
            out_specs=[vmem, vmem, vmem],
            scratch_shapes=scratch,
            compiler_params=pltpu.CompilerParams(collective_id=0, has_side_effects=True),
        )(tokens, cotangent, gains, w_gate, w_up, w_down)

        lead = lax.axis_index("segment") == 0
        return jnp.where(lead, early_rows, last_rows), jnp.where(lead, last_rows, back_rows)

    in_specs = (
        P("dp", None),
        P("dp", None),
        P("segment", None),
        P("segment", "dp", "tensor"),
        P("segment", "dp", "tensor"),
        P("segment", "dp", "tensor"),
    )
    out_specs = (P("segment", "dp", None), P("segment", "dp", None))
    return jax.shard_map(body, mesh=mesh, in_specs=in_specs, out_specs=out_specs, check_vma=False)
```

```python
import functools

import jax
import jax.numpy as jnp
from jax import lax
from jax.experimental import pallas as pl
from jax.experimental.pallas import tpu as pltpu
from jax.sharding import PartitionSpec as P

EPSILON = 1e-06
MESH = pl.DeviceIdType.MESH
F32 = jnp.float32
BF16 = jnp.bfloat16
GU_FAR, DH_FAR = False, False
Z = 8
ORDER = (4, 3, -3, 2, -2, 1, -1, 0)


def halves(tiles):
    first = (tiles + 1) // 2
    return ((0, first * 128, 0), (first * 128, (tiles - first) * 128, 1))


def rows_of(block):
    return block.reshape(-1, block.shape[-1])


def kernel(
    sizes,
    tokens_hbm,
    cotangent_hbm,
    gains,
    wg_hbm,
    wu_hbm,
    wd_hbm,
    out_early,
    out_last,
    out_back,
    given,
    blocks,
    gain_all,
    wg,
    wu,
    wd,
    tin,
    pin,
    xg,
    pg,
    pu,
    pd,
    gu_y,
    gu_ring_y,
    gu_ring_z,
    gu_out,
    gu_fin,
    dh_y,
    dh_ring_y,
    dh_ring_z,
    dh_out,
    dh_fin,
    stash_g,
    stash_u,
    dh_sum,
    hid,
    dg,
    du,
    acc,
    t_out,
    t_in,
    made,
    st_out,
    st_in,
    rows_early,
    rows_back,
    rows_last,
    inv,
    w_sem,
    in_sem,
    gu_sem,
    gu_ysem,
    dh_sem,
    dh_ysem,
    ag_sem,
    ag_ysem,
    t_sem,
    p_sem,
    st_sem,
    row_sem,
    fwd_sem,
    go_sem,
):
    dp_count, tensor_count, rows, width, hidden = sizes
    per = dp_count // tensor_count
    tiles = hidden // 128
    cut = ((tiles * 5 + 8) // 9) * 128
    step_cols = 384
    seg = lax.axis_index("segment")
    i = lax.axis_index("dp")
    j = lax.axis_index("tensor")
    y = i // Z
    m = lax.rem(i, Z)
    across = (seg, (1 - y) * Z + m, j)
    partner = (1 - seg, i, j)

    def beside(d, steps):
        return (seg, y * Z + lax.rem(m + (Z - steps if d == 0 else steps), Z), j)

    others = pl.ds(0, dp_count - 1)
    dp_far = sorted(range(1, dp_count), key=lambda r: -min(r % Z, Z - r % Z))
    tensor_far = sorted(range(1, tensor_count), key=lambda r: (r % 2 == 0, -min(r, tensor_count - r)))

    def at(offset):
        return lax.rem(m + offset + Z, Z)

    def dp_peer(r):
        return (seg, lax.rem(i + r, dp_count), j)

    def tensor_at(r):
        return lax.rem(j + r, tensor_count)

    def send(src, dst, send_sem, recv_sem, to):
        copy = pltpu.make_async_remote_copy(
            src_ref=src,
            dst_ref=dst,
            send_sem=send_sem,
            recv_sem=recv_sem,
            device_id=to,
            device_id_type=MESH,
        )
        copy.start()
        return copy

    def arrived(ref, sem):
        pltpu.make_async_copy(ref, ref, sem).wait()

    barrier = pltpu.get_barrier_semaphore()
    for r in dp_far:
        pl.semaphore_signal(barrier, inc=1, device_id=dp_peer(r), device_id_type=MESH)
    for r in range(1, tensor_count):
        pl.semaphore_signal(barrier, inc=1, device_id=(seg, i, tensor_at(r)), device_id_type=MESH)
    pl.semaphore_signal(barrier, inc=1, device_id=partner, device_id_type=MESH)
    loads = [
        pltpu.make_async_copy(src.at[0], dst, w_sem.at[n])
        for n, (src, dst) in enumerate(((wg_hbm, wg), (wu_hbm, wu), (wd_hbm, wd)))
    ]
    early = seg == 0
    late = seg == 1
    take_tokens = pltpu.make_async_copy(tokens_hbm, given, w_sem.at[3])
    take_cotangent = pltpu.make_async_copy(cotangent_hbm, given, w_sem.at[3])

    @pl.when(early)
    def _():
        take_tokens.start()
        take_tokens.wait()

    @pl.when(late)
    def _():
        take_cotangent.start()
        take_cotangent.wait()

    for load in loads:
        load.start()
    for b in range(dp_count):
        span = slice(b * width, (b + 1) * width)
        blocks[b] = given[:, span]
        gain_all[b : b + 1, :] = gains[:, span]
    tin[i] = blocks[i]
    with jax.named_scope("barrier"):
        pl.semaphore_wait(barrier, dp_count - 1 + tensor_count - 1 + 1)

    @pl.when(late)
    def _():
        pl.semaphore_wait(go_sem, 1)

    for r in dp_far:
        to = lax.rem(i + r, dp_count)
        send(blocks.at[to], tin.at[i], in_sem.at[0], in_sem.at[1], (seg, to, j))

    def write_inverse(source):
        def add(b, total):
            v = source[b].astype(F32)
            return total + v * v

        squares = lax.fori_loop(0, dp_count, add, jnp.zeros((rows, width), F32))
        mean = jnp.sum(squares, axis=1, keepdims=True) / (dp_count * width)
        inv[...] = jnp.broadcast_to(lax.rsqrt(mean + EPSILON), (rows, 128))

    def best_span(count, most):
        n = count // 128
        return max(k for k in range(1, n + 1) if n % k == 0 and k * 128 <= most) * 128

    @jax.named_scope("spread")
    def spread(x, weight, out, c0, count):
        span = best_span(count, 1792)

        def one(n, carry):
            c = pl.multiple_of(c0 + n * span, 128)
            v = jnp.dot(x, weight[:, pl.ds(c, span)], preferred_element_type=F32)
            out[:, :, :, pl.ds(c, span)] = v.astype(BF16).reshape(2, Z, rows, span)
            return carry

        if count == span:
            one(0, 0)
        else:
            lax.fori_loop(0, count // span, one, 0)

    @jax.named_scope("fold")
    def fold(left, weight, c0, count, first):
        span = best_span(count, 1152)

        def product(c):
            return lax.dot_general(
                rows_of(left[:, :, :, pl.ds(c, span)]),
                weight[:, pl.ds(c, span)],
                (((1,), (1,)), ((), ())),
                preferred_element_type=F32,
            )

        def one(n, carry):
            acc[...] += product(pl.multiple_of(c0 + n * span, 128))
            return carry

        if first:
            acc[...] = product(c0)
        lax.fori_loop(1 if first else 0, count // span, one, 0)

    class Ring:
        def __init__(self, own, land, pieces, out_sem, sem, far):
            self.own, self.land, self.pieces, self.out_sem, self.sem, self.far = own, land, pieces, out_sem, sem, far
            self.last = {}

        def cols(self, t, d, k):
            c0, w, _ = self.pieces[k]
            lead = (slice(None),) * (len(self.land.shape) - 3)
            return (t, d, *lead, pl.ds(c0, w))

        def push(self, t, d, k, src):
            copy = send(
                src,
                self.land.at[self.cols(t, d, k)],
                self.out_sem,
                self.sem.at[t, d, k],
                beside(d, 2 if self.far and t in (0, 2) else 1),
            )
            self.last[t, d, k] = copy

        def dest(self, t, d):
            return at(t - 4 if d == 0 else 4 - t)

        def free(self, distance, k):
            c0, w, anti = self.pieces[k]
            t = 4 - distance
            for d in (0, 1):
                if t == 0 and d != anti or t == 1 and d == anti and not self.far:
                    continue
                if t == 2 or t == 3 and not self.far:
                    continue
                self.push(t, d, k, self.own(self.dest(t, d), c0, w))

        def step(self, t):
            if self.far:
                self.join(t)
                return
            for k, (c0, w, anti) in enumerate(self.pieces):
                for d in (0, 1):
                    if t == 1 and d != anti:
                        continue
                    self.last[t - 1, d, k].wait_recv()
                    here = self.land.at[self.cols(t - 1, d, k)]
                    here[...] = here[...] + self.own(self.dest(t, d), c0, w)[...]
                    self.push(t, d, k, here)

        def join(self, t):
            if t != 2:
                return
            for k, (c0, w, anti) in enumerate(self.pieces):
                for d in (0, 1):
                    self.last[1, d, k].wait_recv()
                    here = self.land.at[self.cols(1, d, k)]
                    total = here[...].astype(F32) + self.own(self.dest(2, d), c0, w)[...].astype(F32)
                    if d == anti:
                        self.last[0, d, k].wait_recv()
                        total = total + self.land[self.cols(0, d, k)].astype(F32)
                    here[...] = total.astype(BF16)
                    self.push(2, d, k, here)

        def finish(self, k):
            for d in (0, 1):
                self.last[3, d, k].wait_recv()
                if self.far:
                    self.last[2, d, k].wait_recv()

    def ring_total(land, far, *index):
        total = land[(3, 0, *index)].astype(F32) + land[(3, 1, *index)].astype(F32)
        if far:
            total = total + land[(2, 0, *index)].astype(F32) + land[(2, 1, *index)].astype(F32)
        return total

    def reduce_scatter(py, y0, wy, pz, z0, wz, by, ring_y, ring_z, z_out, z_fin, sem, ysem, fill_y, fill_z, aside, far):
        over_z = Ring(
            lambda dest, c0, w: pz.at[:, dest, :, pl.ds(z0 + c0, w)], ring_z, halves(wz // 128), ysem.at[1], sem.at[0], far
        )
        over_y = Ring(
            lambda dest, c0, w: by.at[dest, :, pl.ds(c0, w)], ring_y, halves(wy // 128), ysem.at[2], sem.at[1], far
        )
        for k, (c0, w, _) in enumerate(over_z.pieces):
            fill_z(z0 + c0, w)
            for distance in (4, 3, 1):
                over_z.free(distance, k)
        for c0, w, _ in over_y.pieces:
            fill_y(y0 + c0, w)
        swaps = [
            send(
                py.at[1 - y, at(off), :, pl.ds(y0, wy)],
                by.at[at(off)],
                ysem.at[0],
                ysem.at[5 + n],
                across,
            )
            for n, off in enumerate(ORDER)
        ]

        def pair(n):
            swaps[n].wait_recv()
            zd = at(ORDER[n])
            by[zd] = by[zd] + py[y, zd, :, pl.ds(y0, wy)]

        aside()

        def step_z(t):
            with jax.named_scope("z%d" % t):
                over_z.step(t)

        def step_y(t):
            with jax.named_scope("y%d" % t):
                over_y.step(t)

        step_z(1)
        pair(0)
        for k in (0, 1):
            over_y.free(4, k)
        step_z(2)
        pair(1)
        pair(2)
        for k in (0, 1):
            over_y.free(3, k)
        step_y(1)
        step_z(3)
        pair(3)
        pair(4)
        step_y(2)
        for k, (c0, w, _) in enumerate(over_z.pieces):
            with jax.named_scope("zf"):
                over_z.finish(k)
            cols = pl.ds(c0, w)
            z_out[:, cols] = (
                pz[1 - y, m, :, pl.ds(z0 + c0, w)].astype(F32)
                + ring_total(ring_z, far, 1 - y, slice(None), cols)
            ).astype(BF16)
            send(z_out.at[:, cols], z_fin.at[:, cols], ysem.at[3], ysem.at[4], across)
        pair(5)
        pair(6)
        for k in (0, 1):
            over_y.free(1, k)
        step_y(3)
        pair(7)
        with jax.named_scope("yf"):
            over_y.finish(0)
            over_y.finish(1)
        with jax.named_scope("last"):
            arrived(z_fin, ysem.at[4])
        arrived(by, ysem.at[0])
        arrived(pz.at[:, pl.ds(0, 7), :, pl.ds(z0, wz)], ysem.at[1])
        arrived(by.at[pl.ds(0, 7)], ysem.at[2])
        arrived(z_out, ysem.at[3])

    def y_total(by, ring_y, c, span, far):
        cols = pl.ds(c, span)
        return by[m, :, cols].astype(F32) + ring_total(ring_y, far, slice(None), cols)

    def z_total(pz, z0, ring_z, z_fin, c, span, far):
        cols = pl.ds(c, span)
        return (
            pz[y, m, :, pl.ds(z0 + c, span)].astype(F32)
            + ring_total(ring_z, far, y, slice(None), cols)
            + z_fin[:, cols].astype(F32)
        )

    @jax.named_scope("rs_dh")
    def scatter_hidden_grads(source, aside):
        x = rows_of(source[...])
        reduce_scatter(
            pd, 0, cut, pd, cut, hidden - cut, dh_y, dh_ring_y, dh_ring_z, dh_out, dh_fin, dh_sem, dh_ysem,
            lambda c, w: spread(x, wd, pd, c, w),
            lambda c, w: spread(x, wd, pd, c, w),
            aside,
            DH_FAR,
        )
        dh_sum[:, pl.ds(0, cut)] = y_total(dh_y, dh_ring_y, 0, cut, DH_FAR)
        dh_sum[:, pl.ds(cut, hidden - cut)] = z_total(pd, cut, dh_ring_z, dh_fin, 0, hidden - cut, DH_FAR)

    def gather_steps(a, a0, wa, b, b0, wb, sem, ysem):
        ca, cb = pl.ds(a0, wa), pl.ds(b0, wb)
        over_a, over_b = {}, {}
        other = 1 - y

        def part(c0, w, k):
            h0, hw, _ = halves(w // 128)[k]
            return pl.ds(c0 + h0, hw)

        def push_a(t, d, k, origin):
            piece = a.at[y, origin, :, part(a0, wa, k)]
            over_a[t, d, k] = send(piece, piece, ysem.at[0], sem.at[0, t, d, k], beside(d, 1))

        def push_b(t, d, k, yy, origin):
            piece = b.at[yy, origin, :, part(b0, wb, k)]
            n = 1 if yy is y else 2
            over_b[n, t, d, k] = send(piece, piece, ysem.at[1], sem.at[n, t, d, k], beside(d, 1))

        def cross_a(origin, k):
            piece = a.at[y, origin, :, part(a0, wa, k)]
            send(piece, piece, ysem.at[2], ysem.at[3], across)

        def arrive(t, over, push, *cross):
            for k in (0, 1):
                for d in (0, 1):
                    if t == 4 and d != k:
                        continue
                    over[t - 1, d, k].wait_recv()
                    origin = at(t if d == 0 else -t)
                    if t < 3 or t == 3 and d == k:
                        push(t, d, k, origin)
                    for to in cross:
                        to(origin, k)

        def arrive_a(t):
            with jax.named_scope("A%d" % t):
                arrive(t, over_a, push_a, cross_a)

        def arrive_b(t, yy):
            n = 1 if yy is y else 2
            with jax.named_scope("%s%d" % (" bB"[n], t)):
                arrive(
                    t,
                    {key[1:]: copy for key, copy in over_b.items() if key[0] == n},
                    lambda t, d, k, origin: push_b(t, d, k, yy, origin),
                )

        mine = b.at[y, m, :, cb]
        first = send(mine, mine, ysem.at[4], ysem.at[5], across)
        for k in (0, 1):
            for d in (0, 1):
                push_a(0, d, k, m)
        for k in (0, 1):
            for d in (0, 1):
                push_b(0, d, k, y, m)
        for k in (0, 1):
            cross_a(m, k)
        yield 0
        for t in (1, 2, 3, 4):
            arrive_a(t)
            if t == 1:
                with jax.named_scope("first"):
                    first.wait_recv()
                for k in (0, 1):
                    for d in (0, 1):
                        push_b(0, d, k, other, m)
            else:
                arrive_b(t - 1, other)
            if t < 4:
                arrive_b(t, y)
                yield t
        with jax.named_scope("cross"):
            arrived(a.at[0, :, :, ca], ysem.at[3])
        yield 4
        arrive_b(4, y)
        arrive_b(4, other)
        yield 5

    def advance(steps, to):
        while next(steps) != to:
            pass

    def gathered(a, a0, wa, b, b0, wb, ysem):
        ca, cb = pl.ds(a0, wa), pl.ds(b0, wb)
        arrived(a.at[0, pl.ds(0, 7), :, ca], ysem.at[0])
        arrived(b.at[:, pl.ds(0, 7), :, cb], ysem.at[1])
        arrived(a.at[0, :, :, ca], ysem.at[2])
        arrived(b.at[0, 0, :, cb], ysem.at[4])

    def row_block(turn, jd, q):
        if turn == 0 or per != 2:
            return per * jd + q
        return lax.rem(i + jd if q == 0 else i - 1 - jd + dp_count, dp_count)

    def tensor_send(turn):
        t_out[turn] = acc[...].reshape(dp_count, rows, width).astype(BF16)
        for r in tensor_far:
            jd = tensor_at(r)
            for q in range(per):
                send(
                    t_out.at[turn, row_block(turn, jd, q)],
                    t_in.at[turn, r - 1, q],
                    t_sem.at[turn, 0],
                    t_sem.at[turn, 1],
                    (seg, i, jd),
                )

    @jax.named_scope("tsum")
    def tensor_sum(turn):
        arrived(t_in.at[turn], t_sem.at[turn, 1])
        totals = [t_out[turn, row_block(turn, j, q)].astype(F32) for q in range(per)]
        for r in range(1, tensor_count):
            for q in range(per):
                totals[q] = totals[q] + t_in[turn, r - 1, q].astype(F32)
        return totals

    def to_partner_segment(src):
        for r in (*tensor_far, 0):
            send(src, pin.at[pl.ds(per * j, per)], p_sem.at[0], p_sem.at[1], (1 - seg, i, tensor_at(r)))

    @jax.named_scope("wait_seg")
    def from_partner_segment():
        arrived(pin, p_sem.at[1])

    @jax.named_scope("exchange")
    def exchange(land, kind):
        land[i] = pin[i]
        for r in dp_far:
            send(pin.at[lax.rem(i + r, dp_count)], land.at[i], row_sem.at[kind, 0], row_sem.at[kind, 1], dp_peer(r))

    @jax.named_scope("exchanged")
    def exchanged(land, kind):
        arrived(land.at[others], row_sem.at[kind, 1])

    def mine_too(q):
        return row_block(1, j, q) == i

    @jax.named_scope("to_rows")
    def to_rows(src, land):
        for r in (*tensor_far, 0):
            for q in range(per):
                to = (seg, row_block(1, j, q), tensor_at(r))
                out, into = row_sem.at[2, 0], row_sem.at[2, 1]
                if r > 0:
                    send(src.at[q], land.at[i], out, into, to)
                    continue

                @pl.when(mine_too(q))
                def _():
                    land[i] = src[q]

                @pl.when(jnp.logical_not(mine_too(q)))
                def _():
                    send(src.at[q], land.at[i], out, into, to)

    def rows_done(land, n):
        own = mine_too(0)
        for q in range(1, per):
            own = jnp.logical_or(own, mine_too(q))

        @pl.when(own)
        def _():
            arrived(land.at[others], row_sem.at[2, n])

        @pl.when(jnp.logical_not(own))
        def _():
            arrived(land, row_sem.at[2, n])

    @jax.named_scope("rows_wait")
    def rows_arrived(land):
        rows_done(land, 1)

    here = pl.ds(per * j, per)
    gain_row = gain_all[pl.ds(i, 1), :]

    with jax.named_scope("entry_wait"):
        arrived(tin.at[others], in_sem.at[1])

    def scale(source):
        xg[...] = (rows_of(source[...]).astype(F32) * gain_row).astype(BF16)

    @pl.when(early)
    def _():
        pl.semaphore_signal(go_sem, inc=1, device_id=partner, device_id_type=MESH)
        scale(tin)

    @pl.when(late)
    def _():
        loads[2].wait()
        pl.semaphore_wait(go_sem, 1)
        scatter_hidden_grads(tin, lambda: None)
        from_partner_segment()
        scale(pin)

    loads[0].wait()
    loads[1].wait()

    def hand_early_rows():
        @pl.when(late)
        def _():
            exchange(rows_early, 0)

    def drain_exchange(land, kind):
        arrived(land.at[others], row_sem.at[kind, 0])

    with jax.named_scope("rs_gu"):
        reduce_scatter(
            pg, 0, hidden, pu, 0, hidden, gu_y, gu_ring_y, gu_ring_z, gu_out, gu_fin, gu_sem, gu_ysem,
            lambda c, w: spread(xg[...], wg, pg, c, w),
            lambda c, w: spread(xg[...], wu, pu, c, w),
            hand_early_rows,
            GU_FAR,
        )

    @pl.when(early)
    def _():
        write_inverse(blocks)

    @pl.when(late)
    def _():
        exchanged(rows_early, 0)
        write_inverse(rows_early)

    def activate(n, carry):
        c = pl.multiple_of(n * step_cols, 128)
        cols = pl.ds(c, step_cols)
        factor = inv[:, 0:1]
        gate = factor * y_total(gu_y, gu_ring_y, c, step_cols, GU_FAR)
        up = factor * z_total(pu, 0, gu_ring_z, gu_fin, c, step_cols, GU_FAR)
        stash_g[:, cols] = gate.astype(BF16)
        stash_u[:, cols] = up.astype(BF16)
        hid[y, m, :, cols] = (gate * jax.nn.sigmoid(gate) * up).astype(BF16)
        return carry

    lax.fori_loop(0, hidden // step_cols, activate, 0)

    def put_rows(out, source):
        for b in range(dp_count):
            out[0, :, b * width : (b + 1) * width] = source[b]

    def write_hidden_grads():
        def one(n, carry):
            c = pl.multiple_of(n * step_cols, 128)
            cols = pl.ds(c, step_cols)
            g = stash_g[:, cols].astype(F32)
            u = stash_u[:, cols].astype(F32)
            d = dh_sum[:, cols]
            s = jax.nn.sigmoid(g)
            dg[y, m, :, cols] = (d * u * s * (1.0 + g * (1.0 - s))).astype(BF16)
            du[y, m, :, cols] = (d * g * s).astype(BF16)
            return carry

        lax.fori_loop(0, hidden // step_cols, one, 0)

    a_cols = cut
    b_cols = hidden - cut

    hid_args = (hid, 0, a_cols, hid, a_cols, b_cols)
    dgu_args = (dg, 0, hidden, du, 0, hidden)

    def start_hidden():
        return gather_steps(*hid_args, ag_sem.at[0], ag_ysem.at[0])

    @jax.named_scope("ag_hid")
    def finish_hidden(steps):
        advance(steps, 4)
        fold(hid, wd, 0, a_cols, True)
        advance(steps, 5)
        fold(hid, wd, a_cols, b_cols, False)

    @jax.named_scope("ag_dgu")
    def gather_hidden_grads(beside_fold):
        steps = gather_steps(*dgu_args, ag_sem.at[1], ag_ysem.at[1])
        advance(steps, 4)
        beside_fold()
        fold(dg, wg, 0, hidden, True)
        advance(steps, 5)
        fold(du, wu, 0, hidden, False)

    @pl.when(early)
    def _():
        loads[2].wait()
        pl.semaphore_signal(go_sem, inc=1, device_id=partner, device_id_type=MESH)
        finish_hidden(start_hidden())
        tensor_send(0)
        totals = tensor_sum(0)
        for q in range(per):
            made[0, q] = (tin[row_block(0, j, q)].astype(F32) + totals[q]).astype(BF16)
        to_partner_segment(made.at[0])
        from_partner_segment()
        scatter_hidden_grads(pin, lambda: None)
        write_hidden_grads()
        gather_hidden_grads(lambda: None)
        pl.semaphore_signal(go_sem, inc=1, device_id=partner, device_id_type=MESH)
        tensor_send(1)
        exchange(rows_back, 1)
        totals = tensor_sum(1)
        for q in range(per):
            made[1, q] = totals[q].astype(BF16)
        to_rows(made.at[1], rows_last)
        exchanged(rows_back, 1)
        back = send(rows_back, rows_back, fwd_sem.at[0, 1], fwd_sem.at[1, 1], partner)
        arrived(rows_early, fwd_sem.at[1, 0])
        put_rows(out_early, rows_early)
        put_rows(out_back, rows_back)
        rows_arrived(rows_last)
        factor = inv[:, 0:1]
        project = jnp.zeros((rows, width), F32)
        for b in range(dp_count):
            weighted = rows_last[b].astype(F32) * gain_all[b : b + 1, :]
            project = project + weighted * (blocks[b].astype(F32) * factor)
        mean = jnp.sum(project, axis=1, keepdims=True) / (dp_count * width)
        for b in range(dp_count):
            weighted = rows_last[b].astype(F32) * gain_all[b : b + 1, :]
            unit = blocks[b].astype(F32) * factor
            out_last[0, :, b * width : (b + 1) * width] = (rows_back[b].astype(F32) + factor * (weighted - unit * mean)).astype(BF16)
        back.wait_send()
        drain_exchange(rows_back, 1)

    @pl.when(late)
    def _():
        write_hidden_grads()
        steps = start_hidden()
        gather_hidden_grads(lambda: advance(steps, 0))
        tensor_send(0)
        advance(steps, 1)
        totals = tensor_sum(0)
        weighted = jnp.concatenate(totals, axis=0) * gain_row
        e = rows_of(pin[here]).astype(F32)
        count = per * rows
        both = jnp.concatenate([weighted * e, e * e], axis=0)
        st_out[...] = jnp.zeros_like(st_out)
        st_out[:, pl.ds(0, 2 * count)] = lax.dot_general(
            jnp.ones((8, width), F32),
            both,
            (((1,), (1,)), ((), ())),
            preferred_element_type=F32,
            precision=lax.Precision.HIGHEST,
        )
        for r in dp_far:
            send(st_out, st_in.at[r], st_sem.at[0], st_sem.at[1], dp_peer(r))
        advance(steps, 2)
        with jax.named_scope("st"):
            arrived(st_in.at[pl.ds(1, dp_count - 1)], st_sem.at[1])
        tally = st_out[...]
        for r in range(1, dp_count):
            tally = tally + st_in[r]
        turned = tally.T
        dot_e = turned[0:count, 0:1] / (dp_count * width)
        squares = turned[count : 2 * count, 0:1] / (dp_count * width)
        factor = lax.rsqrt(squares + EPSILON)
        c = rows_of(tin[here]).astype(F32)
        d_in = c + factor * (weighted - e * factor * (factor * dot_e))
        made[0] = d_in.astype(BF16).reshape(per, rows, width)
        to_partner_segment(made.at[0])
        finish_hidden(steps)
        tensor_send(1)
        totals = tensor_sum(1)
        for q in range(per):
            made[1, q] = (pin[row_block(1, j, q)].astype(F32) + totals[q]).astype(BF16)
        pl.semaphore_wait(go_sem, 1)
        to_rows(made.at[1], rows_last)
        ahead = send(rows_early, rows_early, fwd_sem.at[0, 0], fwd_sem.at[1, 0], partner)
        arrived(rows_back, fwd_sem.at[1, 1])
        put_rows(out_early, rows_early)
        put_rows(out_back, rows_back)
        rows_arrived(rows_last)
        put_rows(out_last, rows_last)
        ahead.wait_send()
        drain_exchange(rows_early, 0)
        arrived(st_in.at[pl.ds(1, dp_count - 1)], st_sem.at[0])

    gathered(*hid_args, ag_ysem.at[0])
    gathered(*dgu_args, ag_ysem.at[1])
    for turn in (0, 1):
        arrived(t_in.at[turn], t_sem.at[turn, 0])
    arrived(pin, p_sem.at[0])
    rows_done(rows_last, 0)
    arrived(blocks.at[others], in_sem.at[0])


def solution(mesh):
    dp_count, tensor_count = mesh.shape["dp"], mesh.shape["tensor"]

    def body(tokens, cotangent, gains, w_gate, w_up, w_down):
        rows, model = tokens.shape
        _, width, hidden = w_gate.shape
        per = dp_count // tensor_count
        tiles = hidden // 128
        cut = ((tiles * 5 + 8) // 9) * 128
        rest = hidden - cut
        def buf(*shape, dtype=BF16):
            return pltpu.VMEM(shape, dtype)

        block = (dp_count, rows, width)
        wide = (2, Z, rows, hidden)
        dma = pltpu.SemaphoreType.DMA
        scratch = [
            buf(rows, model),
            buf(*block),
            buf(dp_count, width, dtype=F32),
            buf(width, hidden),
            buf(width, hidden),
            buf(width, hidden),
            buf(*block),
            buf(*block),
            buf(dp_count * rows, width),
            buf(*wide),
            buf(*wide),
            buf(*wide),
            buf(Z, rows, hidden),
            buf(4, 2, rows, hidden),
            buf(4, 2, 2, rows, hidden),
            buf(rows, hidden),
            buf(rows, hidden),
            buf(Z, rows, cut),
            buf(4, 2, rows, cut),
            buf(4, 2, 2, rows, rest),
            buf(rows, rest),
            buf(rows, rest),
            buf(rows, hidden),
            buf(rows, hidden),
            buf(rows, hidden, dtype=F32),
            buf(*wide),
            buf(*wide),
            buf(*wide),
            buf(dp_count * rows, width, dtype=F32),
            buf(2, *block),
            buf(2, tensor_count - 1, per, rows, width),
            buf(2, per, rows, width),
            buf(8, 128, dtype=F32),
            buf(dp_count, 8, 128, dtype=F32),
            buf(*block),
            buf(*block),
            buf(*block),
            buf(rows, 128, dtype=F32),
            dma((4,)),
            dma((2,)),
            dma((2, 4, 2, 2)),
            dma((5 + Z,)),
            dma((2, 4, 2, 2)),
            dma((5 + Z,)),
            dma((2, 3, 4, 2, 2)),
            dma((2, 6)),
            dma((2, 2)),
            dma((2,)),
            dma((2,)),
            dma((3, 2)),
            dma((2, 2)),
            pltpu.SemaphoreType.REGULAR,
        ]
        vmem = pl.BlockSpec(memory_space=pltpu.VMEM)
        hbm = pl.BlockSpec(memory_space=pl.ANY)
        early_rows, last_rows, back_rows = pl.pallas_call(
            functools.partial(kernel, (dp_count, tensor_count, rows, width, hidden)),
            out_shape=[jax.ShapeDtypeStruct((1, rows, model), BF16)] * 3,
            in_specs=[hbm, hbm, vmem, hbm, hbm, hbm],
            out_specs=[vmem, vmem, vmem],
            scratch_shapes=scratch,
            compiler_params=pltpu.CompilerParams(collective_id=0, has_side_effects=True),
        )(tokens, cotangent, gains, w_gate, w_up, w_down)

        lead = lax.axis_index("segment") == 0
        return jnp.where(lead, early_rows, last_rows), jnp.where(lead, last_rows, back_rows)

    in_specs = (
        P("dp", None),
        P("dp", None),
        P("segment", None),
        P("segment", "dp", "tensor"),
        P("segment", "dp", "tensor"),
        P("segment", "dp", "tensor"),
    )
    out_specs = (P("segment", "dp", None), P("segment", "dp", None))
    return jax.shard_map(body, mesh=mesh, in_specs=in_specs, out_specs=out_specs, check_vma=False)
```

```python
import functools

import jax
import jax.numpy as jnp
from jax import lax
from jax.experimental import pallas as pl
from jax.experimental.pallas import tpu as pltpu
from jax.sharding import PartitionSpec as P

EPSILON = 1e-06
MESH = pl.DeviceIdType.MESH
F32 = jnp.float32
BF16 = jnp.bfloat16
GU_FAR, DH_FAR = False, False
Z = 8
ORDER = (4, 3, -3, 2, -2, 1, -1, 0)


def halves(tiles):
    first = (tiles + 1) // 2
    return ((0, first * 128, 0), (first * 128, (tiles - first) * 128, 1))


def rows_of(block):
    return block.reshape(-1, block.shape[-1])


def kernel(
    sizes,
    tokens_hbm,
    cotangent_hbm,
    gains,
    wg_hbm,
    wu_hbm,
    wd_hbm,
    out_early,
    out_last,
    out_back,
    given,
    blocks,
    gain_all,
    wg,
    wu,
    wd,
    tin,
    pin,
    xg,
    pg,
    pu,
    pd,
    gu_y,
    gu_ring_y,
    gu_ring_z,
    gu_out,
    gu_fin,
    dh_y,
    dh_ring_y,
    dh_ring_z,
    dh_out,
    dh_fin,
    stash_g,
    stash_u,
    dh_sum,
    hid,
    dg,
    du,
    acc,
    t_out,
    t_in,
    made,
    st_out,
    st_in,
    rows_early,
    rows_back,
    rows_last,
    inv,
    w_sem,
    in_sem,
    gu_sem,
    gu_ysem,
    dh_sem,
    dh_ysem,
    ag_sem,
    ag_ysem,
    t_sem,
    p_sem,
    st_sem,
    row_sem,
    fwd_sem,
    go_sem,
):
    dp_count, tensor_count, rows, width, hidden = sizes
    per = dp_count // tensor_count
    tiles = hidden // 128
    cut = ((tiles * 5 + 8) // 9) * 128
    step_cols = 384
    seg = lax.axis_index("segment")
    i = lax.axis_index("dp")
    j = lax.axis_index("tensor")
    y = i // Z
    m = lax.rem(i, Z)
    across = (seg, (1 - y) * Z + m, j)
    partner = (1 - seg, i, j)

    def beside(d, steps):
        return (seg, y * Z + lax.rem(m + (Z - steps if d == 0 else steps), Z), j)

    others = pl.ds(0, dp_count - 1)
    dp_far = sorted(range(1, dp_count), key=lambda r: -min(r % Z, Z - r % Z))
    tensor_far = sorted(range(1, tensor_count), key=lambda r: (r % 2 == 0, -min(r, tensor_count - r)))

    def at(offset):
        return lax.rem(m + offset + Z, Z)

    def dp_peer(r):
        return (seg, lax.rem(i + r, dp_count), j)

    def tensor_at(r):
        return lax.rem(j + r, tensor_count)

    def send(src, dst, send_sem, recv_sem, to):
        copy = pltpu.make_async_remote_copy(
            src_ref=src,
            dst_ref=dst,
            send_sem=send_sem,
            recv_sem=recv_sem,
            device_id=to,
            device_id_type=MESH,
        )
        copy.start()
        return copy

    def arrived(ref, sem):
        pltpu.make_async_copy(ref, ref, sem).wait()

    barrier = pltpu.get_barrier_semaphore()
    for r in dp_far:
        pl.semaphore_signal(barrier, inc=1, device_id=dp_peer(r), device_id_type=MESH)
    for r in range(1, tensor_count):
        pl.semaphore_signal(barrier, inc=1, device_id=(seg, i, tensor_at(r)), device_id_type=MESH)
    pl.semaphore_signal(barrier, inc=1, device_id=partner, device_id_type=MESH)
    loads = [
        pltpu.make_async_copy(src.at[0], dst, w_sem.at[n])
        for n, (src, dst) in enumerate(((wg_hbm, wg), (wu_hbm, wu), (wd_hbm, wd)))
    ]
    early = seg == 0
    late = seg == 1
    take_tokens = pltpu.make_async_copy(tokens_hbm, given, w_sem.at[3])
    take_cotangent = pltpu.make_async_copy(cotangent_hbm, given, w_sem.at[3])

    @pl.when(early)
    def _():
        take_tokens.start()
        take_tokens.wait()

    @pl.when(late)
    def _():
        take_cotangent.start()
        take_cotangent.wait()

    for load in loads:
        load.start()
    for b in range(dp_count):
        span = slice(b * width, (b + 1) * width)
        blocks[b] = given[:, span]
        gain_all[b : b + 1, :] = gains[:, span]
    tin[i] = blocks[i]
    with jax.named_scope("barrier"):
        pl.semaphore_wait(barrier, dp_count - 1 + tensor_count - 1 + 1)

    @pl.when(late)
    def _():
        pl.semaphore_wait(go_sem, 1)

    for r in dp_far:
        to = lax.rem(i + r, dp_count)
        send(blocks.at[to], tin.at[i], in_sem.at[0], in_sem.at[1], (seg, to, j))

    def write_inverse(source):
        def add(b, total):
            v = source[b].astype(F32)
            return total + v * v

        squares = lax.fori_loop(0, dp_count, add, jnp.zeros((rows, width), F32))
        mean = jnp.sum(squares, axis=1, keepdims=True) / (dp_count * width)
        inv[...] = jnp.broadcast_to(lax.rsqrt(mean + EPSILON), (rows, 128))

    def best_span(count, most):
        n = count // 128
        return max(k for k in range(1, n + 1) if n % k == 0 and k * 128 <= most) * 128

    @jax.named_scope("spread")
    def spread(x, weight, out, c0, count):
        span = best_span(count, 1792)

        def one(n, carry):
            c = pl.multiple_of(c0 + n * span, 128)
            v = jnp.dot(x, weight[:, pl.ds(c, span)], preferred_element_type=F32)
            out[:, :, :, pl.ds(c, span)] = v.astype(BF16).reshape(2, Z, rows, span)
            return carry

        if count == span:
            one(0, 0)
        else:
            lax.fori_loop(0, count // span, one, 0)

    @jax.named_scope("fold")
    def fold(left, weight, c0, count, first):
        span = best_span(count, 1152)

        def product(c):
            return lax.dot_general(
                rows_of(left[:, :, :, pl.ds(c, span)]),
                weight[:, pl.ds(c, span)],
                (((1,), (1,)), ((), ())),
                preferred_element_type=F32,
            )

        def one(n, carry):
            acc[...] += product(pl.multiple_of(c0 + n * span, 128))
            return carry

        if first:
            acc[...] = product(c0)
        lax.fori_loop(1 if first else 0, count // span, one, 0)

    class Ring:
        def __init__(self, own, land, pieces, out_sem, sem, far):
            self.own, self.land, self.pieces, self.out_sem, self.sem, self.far = own, land, pieces, out_sem, sem, far
            self.last = {}

        def cols(self, t, d, k):
            c0, w, _ = self.pieces[k]
            lead = (slice(None),) * (len(self.land.shape) - 3)
            return (t, d, *lead, pl.ds(c0, w))

        def push(self, t, d, k, src):
            copy = send(
                src,
                self.land.at[self.cols(t, d, k)],
                self.out_sem,
                self.sem.at[t, d, k],
                beside(d, 2 if self.far and t in (0, 2) else 1),
            )
            self.last[t, d, k] = copy

        def dest(self, t, d):
            return at(t - 4 if d == 0 else 4 - t)

        def free(self, distance, k):
            c0, w, anti = self.pieces[k]
            t = 4 - distance
            for d in (0, 1):
                if t == 0 and d != anti or t == 1 and d == anti and not self.far:
                    continue
                if t == 2 or t == 3 and not self.far:
                    continue
                self.push(t, d, k, self.own(self.dest(t, d), c0, w))

        def step(self, t):
            if self.far:
                self.join(t)
                return
            for k, (c0, w, anti) in enumerate(self.pieces):
                for d in (0, 1):
                    if t == 1 and d != anti:
                        continue
                    self.last[t - 1, d, k].wait_recv()
                    here = self.land.at[self.cols(t - 1, d, k)]
                    here[...] = here[...] + self.own(self.dest(t, d), c0, w)[...]
                    self.push(t, d, k, here)

        def join(self, t):
            if t != 2:
                return
            for k, (c0, w, anti) in enumerate(self.pieces):
                for d in (0, 1):
                    self.last[1, d, k].wait_recv()
                    here = self.land.at[self.cols(1, d, k)]
                    total = here[...].astype(F32) + self.own(self.dest(2, d), c0, w)[...].astype(F32)
                    if d == anti:
                        self.last[0, d, k].wait_recv()
                        total = total + self.land[self.cols(0, d, k)].astype(F32)
                    here[...] = total.astype(BF16)
                    self.push(2, d, k, here)

        def finish(self, k):
            for d in (0, 1):
                self.last[3, d, k].wait_recv()
                if self.far:
                    self.last[2, d, k].wait_recv()

    def ring_total(land, far, *index):
        total = land[(3, 0, *index)].astype(F32) + land[(3, 1, *index)].astype(F32)
        if far:
            total = total + land[(2, 0, *index)].astype(F32) + land[(2, 1, *index)].astype(F32)
        return total

    def reduce_scatter(py, y0, wy, pz, z0, wz, by, ring_y, ring_z, z_out, z_fin, sem, ysem, fill_y, fill_z, aside, far):
        over_z = Ring(
            lambda dest, c0, w: pz.at[:, dest, :, pl.ds(z0 + c0, w)], ring_z, halves(wz // 128), ysem.at[1], sem.at[0], far
        )
        over_y = Ring(
            lambda dest, c0, w: by.at[dest, :, pl.ds(c0, w)], ring_y, halves(wy // 128), ysem.at[2], sem.at[1], far
        )
        for k, (c0, w, _) in enumerate(over_z.pieces):
            fill_z(z0 + c0, w)
            for distance in (4, 3, 1):
                over_z.free(distance, k)
        for c0, w, _ in over_y.pieces:
            fill_y(y0 + c0, w)
        swaps = [
            send(
                py.at[1 - y, at(off), :, pl.ds(y0, wy)],
                by.at[at(off)],
                ysem.at[0],
                ysem.at[5 + n],
                across,
            )
            for n, off in enumerate(ORDER)
        ]

        def pair(n):
            swaps[n].wait_recv()
            zd = at(ORDER[n])
            by[zd] = by[zd] + py[y, zd, :, pl.ds(y0, wy)]

        aside()

        def step_z(t):
            with jax.named_scope("z%d" % t):
                over_z.step(t)

        def step_y(t):
            with jax.named_scope("y%d" % t):
                over_y.step(t)

        step_z(1)
        pair(0)
        for k in (0, 1):
            over_y.free(4, k)
        step_z(2)
        pair(1)
        pair(2)
        for k in (0, 1):
            over_y.free(3, k)
        step_y(1)
        step_z(3)
        pair(3)
        pair(4)
        step_y(2)
        for k, (c0, w, _) in enumerate(over_z.pieces):
            with jax.named_scope("zf"):
                over_z.finish(k)
            cols = pl.ds(c0, w)
            z_out[:, cols] = (
                pz[1 - y, m, :, pl.ds(z0 + c0, w)].astype(F32)
                + ring_total(ring_z, far, 1 - y, slice(None), cols)
            ).astype(BF16)
            send(z_out.at[:, cols], z_fin.at[:, cols], ysem.at[3], ysem.at[4], across)
        pair(5)
        pair(6)
        for k in (0, 1):
            over_y.free(1, k)
        step_y(3)
        pair(7)
        with jax.named_scope("yf"):
            over_y.finish(0)
            over_y.finish(1)
        with jax.named_scope("last"):
            arrived(z_fin, ysem.at[4])
        arrived(by, ysem.at[0])
        arrived(pz.at[:, pl.ds(0, 7), :, pl.ds(z0, wz)], ysem.at[1])
        arrived(by.at[pl.ds(0, 7)], ysem.at[2])
        arrived(z_out, ysem.at[3])

    def y_total(by, ring_y, c, span, far):
        cols = pl.ds(c, span)
        return by[m, :, cols].astype(F32) + ring_total(ring_y, far, slice(None), cols)

    def z_total(pz, z0, ring_z, z_fin, c, span, far):
        cols = pl.ds(c, span)
        return (
            pz[y, m, :, pl.ds(z0 + c, span)].astype(F32)
            + ring_total(ring_z, far, y, slice(None), cols)
            + z_fin[:, cols].astype(F32)
        )

    @jax.named_scope("rs_dh")
    def scatter_hidden_grads(source, aside):
        x = rows_of(source[...])
        reduce_scatter(
            pd, 0, cut, pd, cut, hidden - cut, dh_y, dh_ring_y, dh_ring_z, dh_out, dh_fin, dh_sem, dh_ysem,
            lambda c, w: spread(x, wd, pd, c, w),
            lambda c, w: spread(x, wd, pd, c, w),
            aside,
            DH_FAR,
        )
        dh_sum[:, pl.ds(0, cut)] = y_total(dh_y, dh_ring_y, 0, cut, DH_FAR)
        dh_sum[:, pl.ds(cut, hidden - cut)] = z_total(pd, cut, dh_ring_z, dh_fin, 0, hidden - cut, DH_FAR)

    def gather_steps(a, a0, wa, b, b0, wb, sem, ysem):
        ca, cb = pl.ds(a0, wa), pl.ds(b0, wb)
        over_a, over_b = {}, {}
        other = 1 - y

        def part(c0, w, k):
            h0, hw, _ = halves(w // 128)[k]
            return pl.ds(c0 + h0, hw)

        def push_a(t, d, k, origin):
            piece = a.at[y, origin, :, part(a0, wa, k)]
            over_a[t, d, k] = send(piece, piece, ysem.at[0], sem.at[0, t, d, k], beside(d, 1))

        def push_b(t, d, k, yy, origin):
            piece = b.at[yy, origin, :, part(b0, wb, k)]
            n = 1 if yy is y else 2
            over_b[n, t, d, k] = send(piece, piece, ysem.at[1], sem.at[n, t, d, k], beside(d, 1))

        def cross_a(origin, k):
            piece = a.at[y, origin, :, part(a0, wa, k)]
            send(piece, piece, ysem.at[2], ysem.at[3], across)

        def arrive(t, over, push, *cross):
            for k in (0, 1):
                for d in (0, 1):
                    if t == 4 and d != k:
                        continue
                    over[t - 1, d, k].wait_recv()
                    origin = at(t if d == 0 else -t)
                    if t < 3 or t == 3 and d == k:
                        push(t, d, k, origin)
                    for to in cross:
                        to(origin, k)

        def arrive_a(t):
            with jax.named_scope("A%d" % t):
                arrive(t, over_a, push_a, cross_a)

        def arrive_b(t, yy):
            n = 1 if yy is y else 2
            with jax.named_scope("%s%d" % (" bB"[n], t)):
                arrive(
                    t,
                    {key[1:]: copy for key, copy in over_b.items() if key[0] == n},
                    lambda t, d, k, origin: push_b(t, d, k, yy, origin),
                )

        mine = b.at[y, m, :, cb]
        first = send(mine, mine, ysem.at[4], ysem.at[5], across)
        for k in (0, 1):
            for d in (0, 1):
                push_a(0, d, k, m)
        for k in (0, 1):
            for d in (0, 1):
                push_b(0, d, k, y, m)
        for k in (0, 1):
            cross_a(m, k)
        yield 0
        for t in (1, 2, 3, 4):
            arrive_a(t)
            if t == 1:
                with jax.named_scope("first"):
                    first.wait_recv()
                for k in (0, 1):
                    for d in (0, 1):
                        push_b(0, d, k, other, m)
            else:
                arrive_b(t - 1, other)
            if t < 4:
                arrive_b(t, y)
                yield t
        with jax.named_scope("cross"):
            arrived(a.at[0, :, :, ca], ysem.at[3])
        yield 4
        arrive_b(4, y)
        arrive_b(4, other)
        yield 5

    def advance(steps, to):
        while next(steps) != to:
            pass

    def gathered(a, a0, wa, b, b0, wb, ysem):
        ca, cb = pl.ds(a0, wa), pl.ds(b0, wb)
        arrived(a.at[0, pl.ds(0, 7), :, ca], ysem.at[0])
        arrived(b.at[:, pl.ds(0, 7), :, cb], ysem.at[1])
        arrived(a.at[0, :, :, ca], ysem.at[2])
        arrived(b.at[0, 0, :, cb], ysem.at[4])

    def row_block(turn, jd, q):
        if turn == 0 or per != 2:
            return per * jd + q
        return lax.rem(i + jd if q == 0 else i - 1 - jd + dp_count, dp_count)

    def tensor_send(turn):
        t_out[turn] = acc[...].reshape(dp_count, rows, width).astype(BF16)
        for r in tensor_far:
            jd = tensor_at(r)
            for q in range(per):
                send(
                    t_out.at[turn, row_block(turn, jd, q)],
                    t_in.at[turn, r - 1, q],
                    t_sem.at[turn, 0],
                    t_sem.at[turn, 1],
                    (seg, i, jd),
                )

    @jax.named_scope("tsum")
    def tensor_sum(turn):
        arrived(t_in.at[turn], t_sem.at[turn, 1])
        totals = [t_out[turn, row_block(turn, j, q)].astype(F32) for q in range(per)]
        for r in range(1, tensor_count):
            for q in range(per):
                totals[q] = totals[q] + t_in[turn, r - 1, q].astype(F32)
        return totals

    def to_partner_segment(src):
        for r in (*tensor_far, 0):
            send(src, pin.at[pl.ds(per * j, per)], p_sem.at[0], p_sem.at[1], (1 - seg, i, tensor_at(r)))

    @jax.named_scope("wait_seg")
    def from_partner_segment():
        arrived(pin, p_sem.at[1])

    @jax.named_scope("exchange")
    def exchange(land, kind):
        land[i] = pin[i]
        for r in dp_far:
            send(pin.at[lax.rem(i + r, dp_count)], land.at[i], row_sem.at[kind, 0], row_sem.at[kind, 1], dp_peer(r))

    @jax.named_scope("exchanged")
    def exchanged(land, kind):
        arrived(land.at[others], row_sem.at[kind, 1])

    def mine_too(q):
        return row_block(1, j, q) == i

    @jax.named_scope("to_rows")
    def to_rows(src, land):
        for r in (*tensor_far, 0):
            for q in range(per):
                to = (seg, row_block(1, j, q), tensor_at(r))
                out, into = row_sem.at[2, 0], row_sem.at[2, 1]
                if r > 0:
                    send(src.at[q], land.at[i], out, into, to)
                    continue

                @pl.when(mine_too(q))
                def _():
                    land[i] = src[q]

                @pl.when(jnp.logical_not(mine_too(q)))
                def _():
                    send(src.at[q], land.at[i], out, into, to)

    def rows_done(land, n):
        own = mine_too(0)
        for q in range(1, per):
            own = jnp.logical_or(own, mine_too(q))

        @pl.when(own)
        def _():
            arrived(land.at[others], row_sem.at[2, n])

        @pl.when(jnp.logical_not(own))
        def _():
            arrived(land, row_sem.at[2, n])

    @jax.named_scope("rows_wait")
    def rows_arrived(land):
        rows_done(land, 1)

    here = pl.ds(per * j, per)
    gain_row = gain_all[pl.ds(i, 1), :]

    with jax.named_scope("entry_wait"):
        arrived(tin.at[others], in_sem.at[1])

    def scale(source):
        xg[...] = (rows_of(source[...]).astype(F32) * gain_row).astype(BF16)

    @pl.when(early)
    def _():
        pl.semaphore_signal(go_sem, inc=1, device_id=partner, device_id_type=MESH)
        scale(tin)

    @pl.when(late)
    def _():
        loads[2].wait()
        pl.semaphore_wait(go_sem, 1)
        scatter_hidden_grads(tin, lambda: None)
        from_partner_segment()
        exchange(rows_early, 0)
        scale(pin)

    loads[0].wait()
    loads[1].wait()

    def drain_exchange(land, kind):
        arrived(land.at[others], row_sem.at[kind, 0])

    with jax.named_scope("rs_gu"):
        reduce_scatter(
            pg, 0, hidden, pu, 0, hidden, gu_y, gu_ring_y, gu_ring_z, gu_out, gu_fin, gu_sem, gu_ysem,
            lambda c, w: spread(xg[...], wg, pg, c, w),
            lambda c, w: spread(xg[...], wu, pu, c, w),
            lambda: None,
            GU_FAR,
        )

    @pl.when(early)
    def _():
        write_inverse(blocks)

    @pl.when(late)
    def _():
        exchanged(rows_early, 0)
        write_inverse(rows_early)

    def activate(n, carry):
        c = pl.multiple_of(n * step_cols, 128)
        cols = pl.ds(c, step_cols)
        factor = inv[:, 0:1]
        gate = factor * y_total(gu_y, gu_ring_y, c, step_cols, GU_FAR)
        up = factor * z_total(pu, 0, gu_ring_z, gu_fin, c, step_cols, GU_FAR)
        stash_g[:, cols] = gate.astype(BF16)
        stash_u[:, cols] = up.astype(BF16)
        hid[y, m, :, cols] = (gate * jax.nn.sigmoid(gate) * up).astype(BF16)
        return carry

    lax.fori_loop(0, hidden // step_cols, activate, 0)

    def put_rows(out, source):
        for b in range(dp_count):
            out[0, :, b * width : (b + 1) * width] = source[b]

    def write_hidden_grads():
        def one(n, carry):
            c = pl.multiple_of(n * step_cols, 128)
            cols = pl.ds(c, step_cols)
            g = stash_g[:, cols].astype(F32)
            u = stash_u[:, cols].astype(F32)
            d = dh_sum[:, cols]
            s = jax.nn.sigmoid(g)
            dg[y, m, :, cols] = (d * u * s * (1.0 + g * (1.0 - s))).astype(BF16)
            du[y, m, :, cols] = (d * g * s).astype(BF16)
            return carry

        lax.fori_loop(0, hidden // step_cols, one, 0)

    a_cols = cut
    b_cols = hidden - cut

    hid_args = (hid, 0, a_cols, hid, a_cols, b_cols)
    dgu_args = (dg, 0, hidden, du, 0, hidden)

    def start_hidden():
        return gather_steps(*hid_args, ag_sem.at[0], ag_ysem.at[0])

    @jax.named_scope("ag_hid")
    def finish_hidden(steps):
        advance(steps, 4)
        fold(hid, wd, 0, a_cols, True)
        advance(steps, 5)
        fold(hid, wd, a_cols, b_cols, False)

    @jax.named_scope("ag_dgu")
    def gather_hidden_grads(beside_fold):
        steps = gather_steps(*dgu_args, ag_sem.at[1], ag_ysem.at[1])
        advance(steps, 4)
        beside_fold()
        fold(dg, wg, 0, hidden, True)
        advance(steps, 5)
        fold(du, wu, 0, hidden, False)

    @pl.when(early)
    def _():
        loads[2].wait()
        pl.semaphore_signal(go_sem, inc=1, device_id=partner, device_id_type=MESH)
        finish_hidden(start_hidden())
        tensor_send(0)
        totals = tensor_sum(0)
        for q in range(per):
            made[0, q] = (tin[row_block(0, j, q)].astype(F32) + totals[q]).astype(BF16)
        to_partner_segment(made.at[0])
        from_partner_segment()
        scatter_hidden_grads(pin, lambda: None)
        write_hidden_grads()
        gather_hidden_grads(lambda: None)
        pl.semaphore_signal(go_sem, inc=1, device_id=partner, device_id_type=MESH)
        tensor_send(1)
        exchange(rows_back, 1)
        totals = tensor_sum(1)
        for q in range(per):
            made[1, q] = totals[q].astype(BF16)
        to_rows(made.at[1], rows_last)
        exchanged(rows_back, 1)
        back = send(rows_back, rows_back, fwd_sem.at[0, 1], fwd_sem.at[1, 1], partner)
        arrived(rows_early, fwd_sem.at[1, 0])
        put_rows(out_early, rows_early)
        put_rows(out_back, rows_back)
        rows_arrived(rows_last)
        factor = inv[:, 0:1]
        project = jnp.zeros((rows, width), F32)
        for b in range(dp_count):
            weighted = rows_last[b].astype(F32) * gain_all[b : b + 1, :]
            project = project + weighted * (blocks[b].astype(F32) * factor)
        mean = jnp.sum(project, axis=1, keepdims=True) / (dp_count * width)
        for b in range(dp_count):
            weighted = rows_last[b].astype(F32) * gain_all[b : b + 1, :]
            unit = blocks[b].astype(F32) * factor
            out_last[0, :, b * width : (b + 1) * width] = (rows_back[b].astype(F32) + factor * (weighted - unit * mean)).astype(BF16)
        back.wait_send()
        drain_exchange(rows_back, 1)

    @pl.when(late)
    def _():
        write_hidden_grads()
        steps = start_hidden()
        gather_hidden_grads(lambda: advance(steps, 0))
        tensor_send(0)
        advance(steps, 1)
        totals = tensor_sum(0)
        weighted = jnp.concatenate(totals, axis=0) * gain_row
        e = rows_of(pin[here]).astype(F32)
        count = per * rows
        both = jnp.concatenate([weighted * e, e * e], axis=0)
        st_out[...] = jnp.zeros_like(st_out)
        st_out[:, pl.ds(0, 2 * count)] = lax.dot_general(
            jnp.ones((8, width), F32),
            both,
            (((1,), (1,)), ((), ())),
            preferred_element_type=F32,
            precision=lax.Precision.HIGHEST,
        )
        for r in dp_far:
            send(st_out, st_in.at[r], st_sem.at[0], st_sem.at[1], dp_peer(r))
        advance(steps, 2)
        with jax.named_scope("st"):
            arrived(st_in.at[pl.ds(1, dp_count - 1)], st_sem.at[1])
        tally = st_out[...]
        for r in range(1, dp_count):
            tally = tally + st_in[r]
        turned = tally.T
        dot_e = turned[0:count, 0:1] / (dp_count * width)
        squares = turned[count : 2 * count, 0:1] / (dp_count * width)
        factor = lax.rsqrt(squares + EPSILON)
        c = rows_of(tin[here]).astype(F32)
        d_in = c + factor * (weighted - e * factor * (factor * dot_e))
        made[0] = d_in.astype(BF16).reshape(per, rows, width)
        to_partner_segment(made.at[0])
        finish_hidden(steps)
        tensor_send(1)
        totals = tensor_sum(1)
        for q in range(per):
            made[1, q] = (pin[row_block(1, j, q)].astype(F32) + totals[q]).astype(BF16)
        pl.semaphore_wait(go_sem, 1)
        to_rows(made.at[1], rows_last)
        ahead = send(rows_early, rows_early, fwd_sem.at[0, 0], fwd_sem.at[1, 0], partner)
        arrived(rows_back, fwd_sem.at[1, 1])
        put_rows(out_early, rows_early)
        put_rows(out_back, rows_back)
        rows_arrived(rows_last)
        put_rows(out_last, rows_last)
        ahead.wait_send()
        drain_exchange(rows_early, 0)
        arrived(st_in.at[pl.ds(1, dp_count - 1)], st_sem.at[0])

    gathered(*hid_args, ag_ysem.at[0])
    gathered(*dgu_args, ag_ysem.at[1])
    for turn in (0, 1):
        arrived(t_in.at[turn], t_sem.at[turn, 0])
    arrived(pin, p_sem.at[0])
    rows_done(rows_last, 0)
    arrived(blocks.at[others], in_sem.at[0])


def solution(mesh):
    dp_count, tensor_count = mesh.shape["dp"], mesh.shape["tensor"]

    def body(tokens, cotangent, gains, w_gate, w_up, w_down):
        rows, model = tokens.shape
        _, width, hidden = w_gate.shape
        per = dp_count // tensor_count
        tiles = hidden // 128
        cut = ((tiles * 5 + 8) // 9) * 128
        rest = hidden - cut
        def buf(*shape, dtype=BF16):
            return pltpu.VMEM(shape, dtype)

        block = (dp_count, rows, width)
        wide = (2, Z, rows, hidden)
        dma = pltpu.SemaphoreType.DMA
        scratch = [
            buf(rows, model),
            buf(*block),
            buf(dp_count, width, dtype=F32),
            buf(width, hidden),
            buf(width, hidden),
            buf(width, hidden),
            buf(*block),
            buf(*block),
            buf(dp_count * rows, width),
            buf(*wide),
            buf(*wide),
            buf(*wide),
            buf(Z, rows, hidden),
            buf(4, 2, rows, hidden),
            buf(4, 2, 2, rows, hidden),
            buf(rows, hidden),
            buf(rows, hidden),
            buf(Z, rows, cut),
            buf(4, 2, rows, cut),
            buf(4, 2, 2, rows, rest),
            buf(rows, rest),
            buf(rows, rest),
            buf(rows, hidden),
            buf(rows, hidden),
            buf(rows, hidden, dtype=F32),
            buf(*wide),
            buf(*wide),
            buf(*wide),
            buf(dp_count * rows, width, dtype=F32),
            buf(2, *block),
            buf(2, tensor_count - 1, per, rows, width),
            buf(2, per, rows, width),
            buf(8, 128, dtype=F32),
            buf(dp_count, 8, 128, dtype=F32),
            buf(*block),
            buf(*block),
            buf(*block),
            buf(rows, 128, dtype=F32),
            dma((4,)),
            dma((2,)),
            dma((2, 4, 2, 2)),
            dma((5 + Z,)),
            dma((2, 4, 2, 2)),
            dma((5 + Z,)),
            dma((2, 3, 4, 2, 2)),
            dma((2, 6)),
            dma((2, 2)),
            dma((2,)),
            dma((2,)),
            dma((3, 2)),
            dma((2, 2)),
            pltpu.SemaphoreType.REGULAR,
        ]
        vmem = pl.BlockSpec(memory_space=pltpu.VMEM)
        hbm = pl.BlockSpec(memory_space=pl.ANY)
        early_rows, last_rows, back_rows = pl.pallas_call(
            functools.partial(kernel, (dp_count, tensor_count, rows, width, hidden)),
            out_shape=[jax.ShapeDtypeStruct((1, rows, model), BF16)] * 3,
            in_specs=[hbm, hbm, vmem, hbm, hbm, hbm],
            out_specs=[vmem, vmem, vmem],
            scratch_shapes=scratch,
            compiler_params=pltpu.CompilerParams(collective_id=0, has_side_effects=True),
        )(tokens, cotangent, gains, w_gate, w_up, w_down)

        lead = lax.axis_index("segment") == 0
        return jnp.where(lead, early_rows, last_rows), jnp.where(lead, last_rows, back_rows)

    in_specs = (
        P("dp", None),
        P("dp", None),
        P("segment", None),
        P("segment", "dp", "tensor"),
        P("segment", "dp", "tensor"),
        P("segment", "dp", "tensor"),
    )
    out_specs = (P("segment", "dp", None), P("segment", "dp", None))
    return jax.shard_map(body, mesh=mesh, in_specs=in_specs, out_specs=out_specs, check_vma=False)
```
